128 devices in a mesh: sample: 8 (over x, core), gene: 4 (over y), cohort: 4 (over z).
Axes of the slice: x: 4, y: 4, z: 4, core: 2. Of those that a mesh axis runs over, the one named last changes fastest.
Arguments:
- dosage: bfloat16 [16384, 32768], P(('sample', 'cohort'), 'gene'), may hold values from 0 to 2
- covariates: bfloat16 [16384, 32], P(('sample', 'cohort')), may hold values from 0 to 2
- phenotype: bfloat16 [16384], P(('sample', 'cohort')), may hold values from -6 to 6
- sample_mask: int32 [16384], P(('sample', 'cohort')), may hold values 0 or 1
- variant_weight: float32 [32768], replicated, may hold values from 0.1 to 1
- bucket_owner: int32 [256], replicated, may hold values from 0 to 15, as said below
- variant_gene: int32 [32768], replicated, may hold values from -1 to 127, as said below
Outputs:
- gram_tiles: float32 [16, 16, 128, 128], P(('gene', 'cohort'), 'sample')
- rho_stats: float32 [8, 128], P(None, ('gene', 'cohort'))
- gene_trace: float32 [128], P(('gene', 'cohort'))
The draws below stay inside these ranges and needn't reach their ends.
Inputs may be any that keep to these rules, and one draw needn't show every extreme that they name: `bucket_owner`: every owner holds exactly 16 buckets, at most 8 of them among the 64 buckets of one index of gene, and some owner exactly 8; of the buckets of one index of gene, exactly 16 belong to owners whose index leaves a given remainder on division by the size of the cohort axis. `variant_gene`: genes o * 8 to (o + 1) * 8 - 1 lie in the buckets of owner o, each in one or more whole buckets that are consecutive among that owner's buckets; all its buckets are full but its last, whose first 10 to 128 columns are live and the rest -1.
All inputs are finite; a program needn't handle non-finite values. No bound on the sum of `sample_mask` on one device may be relied on, other than what follows from the above.
Results may differ from the reference program's by a relative error of at most 0.0003.
Values may be sent and summed in bfloat16 or wider, within the bound.
No kernel may reach another device: no remote copies, remote signals or barrier semaphores. Data moves between devices by JAX's collectives and lax.ppermute only.
A program may use at most 128 MiB of HBM per device.

```python
import math
import jax
import jax.numpy as jnp
from jax import lax

B_DEV = 16
COVS = 32
BUCKET_WIDTH = 128
CAP = 8
GENES_OWN = 8
OWNERS = 16
SRC_BUCKETS = 64
BUCKETS = 256
VARIANTS = 32768
GENES = 128
SAMPLES = 16384
N_GENE = 4
N_COHORT = 4


def bucket_layout(key):
    subkeys = jax.random.split(jax.random.fold_in(key, 11), 5)
    rotation = jax.random.randint(subkeys[0], (), 0, N_GENE).astype(jnp.int32)
    owner_ids = jnp.arange(OWNERS, dtype=jnp.int32)
    surplus_at = (owner_ids // N_COHORT + owner_ids % N_COHORT + rotation) % N_GENE
    deficit_at = (surplus_at + 1) % N_GENE
    mean_take = B_DEV // N_GENE
    extra_take = CAP - mean_take
    gene_ids = jnp.arange(N_GENE, dtype=jnp.int32)
    counts = mean_take + extra_take * ((gene_ids[None, :] == surplus_at[:, None]).astype(jnp.int32) - (gene_ids[None, :] == deficit_at[:, None]).astype(jnp.int32))
    running = jnp.cumsum(counts, axis=0)
    position = jnp.arange(SRC_BUCKETS, dtype=jnp.int32)
    labels = jnp.sum((running[:, None, :] <= position[None, :, None]).astype(jnp.int32), axis=0)

    def shuffle_block(block_key, column):
        return jax.random.permutation(block_key, column)
    blocks = jax.vmap(shuffle_block)(jax.random.split(subkeys[1], N_GENE), labels.T)
    owners = blocks.reshape(BUCKETS).astype(jnp.int32)
    onehot = (owners[:, None] == owner_ids[None, :]).astype(jnp.int32)
    owner_rank = jnp.sum((jnp.cumsum(onehot, axis=0) - onehot) * onehot, axis=1)

    def cut_one(cut_key):
        return jnp.sort(jax.random.permutation(cut_key, B_DEV - 1)[:GENES_OWN - 1]) + 1
    cuts = jax.vmap(cut_one)(jax.random.split(subkeys[3], OWNERS)).astype(jnp.int32)
    own_cuts = cuts[owners]
    local_gene = jnp.sum((own_cuts <= owner_rank[:, None]).astype(jnp.int32), axis=1)
    is_last = (owner_rank == B_DEV - 1) | jnp.any(own_cuts == owner_rank[:, None] + 1, axis=1)
    filled = jnp.where(is_last, jax.random.randint(subkeys[4], (BUCKETS,), 10, BUCKET_WIDTH + 1), BUCKET_WIDTH)
    column = jnp.arange(BUCKET_WIDTH, dtype=jnp.int32)
    gene_of = jnp.where(column[None, :] < filled[:, None], (owners * GENES_OWN + local_gene)[:, None], -1)
    return (owners, gene_of.reshape(VARIANTS).astype(jnp.int32))


def draw_bucket_owner(key, part):
    return bucket_layout(key)[0]


def draw_variant_gene(key, part):
    return bucket_layout(key)[1]


def draw_dosage(key, part):
    uniform_base = jax.random.uniform(key, (SAMPLES, VARIANTS + 1), jnp.float32, -1.0, 1.0)
    return (1.0 + 0.6 * uniform_base[:, 1:] + 0.4 * uniform_base[:, :-1]).astype(jnp.bfloat16)


def plant(result, stream_key, least, largest):
    extent = result.shape
    index_at = [jax.random.randint(jax.random.fold_in(stream_key, axis), (), 0, extent[axis]) for axis in range(len(extent))]
    result = result.at[tuple(index_at)].set(least)
    longest = extent.index(max(extent))
    index_at[longest] = (index_at[longest] + 1) % extent[longest]
    return result.at[tuple(index_at)].set(largest)


def shard_levels(stream_key, shape, pieces, smallest, largest):
    gain, own = 1.0, jax.random.fold_in(stream_key, 6)
    for axis_at, shards_of in pieces:
        heights = jnp.exp(jax.random.uniform(jax.random.fold_in(own, axis_at), (shards_of,), jnp.float32, smallest / len(pieces), largest / len(pieces)))
        gain = gain * jnp.repeat(heights, shape[axis_at] // shards_of).reshape([-1 if axis == axis_at else 1 for axis in range(len(shape))])
    return gain


def noise(rng, dims, width, bound, shards=(), kind=jnp.bfloat16):
    result = width * jax.random.normal(rng, dims, jnp.float32)
    if shards:
        result = result * shard_levels(rng, dims, shards, -0.22, 0.18)
    return jnp.clip(result, -bound, bound).astype(kind)


def setup_inputs(seed: int = 0) -> dict:
    streams_of = jax.random.split(jax.random.key(seed), 8)
    return {
        "dosage": draw_dosage(jax.random.fold_in(streams_of[7], 71), 0),
        "covariates": jnp.clip(2.0 * jax.random.uniform(streams_of[1], (SAMPLES, COVS), jnp.float32) ** shard_levels(streams_of[1], (SAMPLES, COVS), ((0, 32),), -0.2, 0.2), 0.0, 2.0).astype(jnp.bfloat16),
        "phenotype": noise(streams_of[2], (SAMPLES,), 1.0, 6.0, ((0, 32),)),
        "sample_mask": plant((jax.random.randint(streams_of[3], (SAMPLES,), 0, 10) < 9).astype(jnp.int32), jax.random.fold_in(streams_of[3], 1), 0, 1),
        "variant_weight": jnp.clip(jnp.exp(jax.random.uniform(streams_of[4], (VARIANTS,), jnp.float32, math.log(0.1), math.log(1.0))), 0.1, 1.0),
        "bucket_owner": draw_bucket_owner(jax.random.fold_in(streams_of[7], 71), 0),
        "variant_gene": draw_variant_gene(jax.random.fold_in(streams_of[7], 71), 0),
    }


RHO_GRID = (0.0, 0.01, 0.04, 0.09, 0.16, 0.25, 0.5, 1.0)

def solve_moments(factor, rhs):
    half = lax.linalg.triangular_solve(factor, rhs, left_side=True, lower=True)
    return lax.linalg.triangular_solve(factor, half, left_side=True, lower=True, transpose_a=True)

def segment_total(values, segment_ids):
    return jax.ops.segment_sum(values, segment_ids, num_segments=GENES + 1)[:GENES]

def reference(dosage, covariates, phenotype, sample_mask, variant_weight, bucket_owner, variant_gene):
    sample_keep = sample_mask.astype(jnp.bfloat16)
    masked_cov = covariates * sample_keep[:, None]
    left_cols = jnp.concatenate([masked_cov, (phenotype * sample_keep)[:, None]], axis=1)
    moments = jnp.dot(masked_cov.T.astype(jnp.float32), jnp.concatenate([covariates, phenotype[:, None]], axis=1).astype(jnp.float32), preferred_element_type=jnp.float32)
    factor = jnp.linalg.cholesky(moments[:, :COVS])
    beta_hat = solve_moments(factor, moments[:, COVS:])[:, 0]

    def bucket_terms(bucket):
        panel_block = lax.dynamic_slice_in_dim(dosage, bucket * BUCKET_WIDTH, BUCKET_WIDTH, 1)
        masked_block = panel_block * sample_keep[:, None]
        gram_part = jnp.dot(masked_block.T.astype(jnp.float32), panel_block.astype(jnp.float32), preferred_element_type=jnp.float32)
        cross_part = jnp.dot(left_cols.T.astype(jnp.float32), panel_block.astype(jnp.float32), preferred_element_type=jnp.float32)
        return (gram_part, cross_part)
    gram_all, cross_all = lax.map(bucket_terms, jnp.arange(BUCKETS, dtype=jnp.int32))
    cov_cross = cross_all[:, :COVS, :]
    raw_score = cross_all[:, COVS, :]
    stacked = jnp.transpose(cov_cross, (1, 0, 2)).reshape(COVS, BUCKETS * BUCKET_WIDTH)
    solved = solve_moments(factor, stacked).reshape(COVS, BUCKETS, BUCKET_WIDTH)
    projected = jnp.einsum('bcj,cbk->bjk', cov_cross, solved, precision=lax.Precision.HIGHEST)
    scores = raw_score - jnp.einsum('bcj,c->bj', cov_cross, beta_hat, precision=lax.Precision.HIGHEST)
    live_weight = jnp.where(variant_gene >= 0, variant_weight, 0.0).reshape(BUCKETS, BUCKET_WIDTH)
    tile_all = live_weight[:, :, None] * live_weight[:, None, :] * (gram_all - projected) / SAMPLES
    zscore = (live_weight * scores / math.sqrt(SAMPLES)).reshape(VARIANTS)
    segment_ids = jnp.where(variant_gene >= 0, variant_gene, GENES)
    squares = segment_total(zscore * zscore, segment_ids)
    burden_sum = segment_total(zscore, segment_ids)
    trace_sum = segment_total(jnp.diagonal(tile_all, axis1=1, axis2=2).reshape(VARIANTS), segment_ids)
    rho_col = jnp.array(RHO_GRID, dtype=jnp.float32)[:, None]
    rho_stats = ((1.0 - rho_col) * squares[None, :] + rho_col * (burden_sum * burden_sum)[None, :]) / BUCKET_WIDTH
    gene_trace = trace_sum / BUCKET_WIDTH
    onehot = (bucket_owner[:, None] == jnp.arange(OWNERS, dtype=jnp.int32)[None, :]).astype(jnp.int32)
    owner_rank = lax.optimization_barrier(jnp.sum((jnp.cumsum(onehot, axis=0) - onehot) * onehot, axis=1))
    slot_order = jnp.zeros((BUCKETS,), jnp.int32).at[bucket_owner * B_DEV + owner_rank].set(jnp.arange(BUCKETS, dtype=jnp.int32))
    gram_tiles = tile_all[slot_order].reshape(OWNERS, B_DEV, BUCKET_WIDTH, BUCKET_WIDTH)
    return (gram_tiles, rho_stats, gene_trace)
```

```python
import jax
import jax.numpy as jnp
from jax import lax
from jax.experimental import pallas as pl
from jax.experimental.pallas import tpu as pltpu
from jax.sharding import Mesh, PartitionSpec as P

AXES = ("x", "k", "g", "c")
RHO_GRID = (0.0, 0.01, 0.04, 0.09, 0.16, 0.25, 0.5, 1.0)
SAMPLES = 16384
WIDTH = 128
COVS = 32
LOCAL = 64
STEP = 4
CHUNK = 208
ROUTED = 112
FINAL = 48
F32 = jnp.float32
HIGHEST = lax.Precision.HIGHEST


def params(**kwargs):
    return pltpu.CompilerParams(vmem_limit_bytes=48 * 1024 * 1024, **kwargs)


def iota(shape, dim):
    return lax.broadcasted_iota(jnp.int32, shape, dim)


def products_kernel(owner_ref, dosage_ref, cov_ref, pheno_ref, mask_ref, keep_ref, send_ref,
                    left_ref, packed_ref, cross_ref, rest_ref, moment_ref, count_ref):
    step = pl.program_id(0)
    x, k, g, c = (lax.axis_index(a) for a in AXES)

    def place(core, xd, cd):
        first = core == 0
        d = jnp.where(first, (xd - x) & 3, (cd - c) & 3)
        j = jnp.where(first, cd, xd)
        return d, j

    @pl.when(step == 0)
    def _():
        rest_ref[...] = jnp.zeros_like(rest_ref)
        for i in range(4):
            count_ref[i] = 0
        cov_rows = cov_ref[...].T
        pheno = pheno_ref[...]
        right = jnp.concatenate(
            [cov_rows, pheno, jnp.zeros((WIDTH - COVS - 1, cov_rows.shape[1]), jnp.bfloat16)], 0)
        keep = mask_ref[...].astype(F32).astype(jnp.bfloat16)
        masked = right[:48] * keep
        left_ref[...] = masked
        m = lax.dot_general(masked[:COVS], right, (((1,), (1,)), ((), ())),
                            preferred_element_type=F32)
        moment_ref[...] = pltpu.roll(m[:16], 32, 1) + pltpu.roll(m[16:32], 65, 1)

    keep_row = mask_ref[...].astype(F32).astype(jnp.bfloat16)
    row, lane = iota((64, WIDTH), 0), iota((64, WIDTH), 1)
    take_low = (lane < 64) & (row > lane)
    eye = iota((WIDTH, WIDTH), 0) == iota((WIDTH, WIDTH), 1)
    for pair in range(STEP // 2):
        panel = dosage_ref[:, pair * 256:(pair + 1) * 256]
        left = jnp.concatenate([panel.T * keep_row, left_ref[...]], 0)
        out = jnp.dot(left, panel, preferred_element_type=F32)
        for half in range(2):
            lo = half * WIDTH
            block = out[lo:lo + WIDTH, lo:lo + WIDTH]
            bucket = step * STEP + pair * 2 + half
            cd = owner_ref[g * LOCAL + bucket] & 3
            pos = count_ref[cd]
            count_ref[cd] = pos + 1
            slot = pair * 2 + half
            packed_ref[slot] = jnp.where(take_low, pltpu.roll(block[64:], 64, 1), block[:64])
            rows = pl.ds(pl.multiple_of(pos * 8, 8), 8)
            for xd in range(4):
                d, j = place(k, xd, cd)
                keep_ref[d, j, rows, :] = packed_ref[
                    slot, pl.ds(pl.multiple_of((2 * xd + k) * 8, 8), 8), :]
                d, j = place(1 - k, xd, cd)
                send_ref[d, j, rows, :] = packed_ref[
                    slot, pl.ds(pl.multiple_of((2 * xd + 1 - k) * 8, 8), 8), :]
            cross_ref[cd, pl.ds(pl.multiple_of(pos * COVS, 8), COVS), :] = out[
                256:256 + COVS, lo:lo + WIDTH]
            rest_ref[cd, pl.ds(pos, 1), :] = out[256 + COVS:257 + COVS, lo:lo + WIDTH]
            rest_ref[cd, pl.ds(pos + 16, 1), :] = jnp.sum(
                jnp.where(eye, block, 0.0), axis=0, keepdims=True)

    @pl.when(step == pl.num_programs(0) - 1)
    def _():
        for cd in range(4):
            for q in range(5):
                if q < 4:
                    turned = cross_ref[cd, q * WIDTH:(q + 1) * WIDTH, :].T
                else:
                    turned = rest_ref[cd].T
                for t in range(8):
                    tile = turned[16 * t:16 * t + 16]
                    if q == 4:
                        tile = tile + moment_ref[...]
                    rows = slice(128 + 16 * q, 144 + 16 * q)
                    d, j = place(t & 1, t >> 1, cd)

                    @pl.when(k == (t & 1))
                    def _():
                        keep_ref[d, j, rows, :] = tile

                    @pl.when(k != (t & 1))
                    def _():
                        send_ref[d, j, rows, :] = tile


def products(owner, dosage, cov, pheno, mask):
    samples = dosage.shape[0]
    out = jax.ShapeDtypeStruct((4, 4, CHUNK, WIDTH), F32)
    whole = lambda shape: pl.BlockSpec(shape, lambda i, o: (0,) * len(shape))
    return pl.pallas_call(
        products_kernel,
        out_shape=(out, out),
        grid_spec=pltpu.PrefetchScalarGridSpec(
            num_scalar_prefetch=1,
            grid=(LOCAL // STEP,),
            in_specs=[
                pl.BlockSpec((samples, STEP * WIDTH), lambda i, o: (0, i)),
                whole(cov.shape), whole(pheno.shape), whole(mask.shape),
            ],
            out_specs=[whole(out.shape), whole(out.shape)],
            scratch_shapes=[
                pltpu.VMEM((48, samples), jnp.bfloat16),
                pltpu.VMEM((STEP, 64, WIDTH), F32),
                pltpu.VMEM((4, 16 * COVS, WIDTH), F32),
                pltpu.VMEM((4, WIDTH, WIDTH), F32),
                pltpu.VMEM((16, WIDTH), F32),
                pltpu.SMEM((4,), jnp.int32),
            ],
        ),
        compiler_params=params(dimension_semantics=("arbitrary",)),
        name="products",
    )(owner, dosage, cov, pheno, mask)


def first_sum_kernel(keep_ref, recv_ref, *outs):
    for d in range(4):
        outs[d][...] = keep_ref[d] + recv_ref[d]


def second_sum_kernel(a0, r1, r2, r3, *outs):
    x, k, g, c = (lax.axis_index(a) for a in AXES)
    base = jnp.where(k == 0, c, x)
    for d in range(4):
        j = (base + d) & 3
        outs[d][...] = (a0[j] + r1[j]) + (r2[j] + r3[j])


def vmem_call(kernel, shapes, name, n_in, scratch=(), smem_in=0, smem_out=()):
    specs = [pl.BlockSpec(memory_space=pltpu.SMEM)] * smem_in + [
        pl.BlockSpec(memory_space=pltpu.VMEM)] * (n_in - smem_in)
    return pl.pallas_call(
        kernel,
        out_shape=tuple(shapes),
        in_specs=specs,
        out_specs=tuple(
            pl.BlockSpec(memory_space=pltpu.SMEM if i in smem_out else pltpu.VMEM)
            for i in range(len(shapes))),
        scratch_shapes=scratch,
        compiler_params=params(),
        name=name,
    )


def route_kernel(owner_ref, b0, q1, q2, q3, e0, e1, e2, e3, moment_ref, total_ref, slot_ref,
                 count_ref):
    x, k, g, c = (lax.axis_index(a) for a in AXES)
    total_ref[...] = (b0[...] + q1[...]) + (q2[...] + q3[...])
    moment_ref[...] = total_ref[192:208, :]
    slot_ref[...] = jnp.zeros_like(slot_ref)
    for i in range(5):
        count_ref[i] = 0
    lane = iota((16, WIDTH), 1)

    def body(bucket, _):
        owner = owner_ref[g * LOCAL + bucket]

        @pl.when((owner & 3) == c)
        def _():
            pos = count_ref[4]
            count_ref[4] = pos + 1
            gd = owner >> 2
            pr = count_ref[gd]
            count_ref[gd] = pr + 1
            d = (gd - g) & 3
            slot_ref[d, pl.ds(pl.multiple_of(pr * 8, 8), 8), :] = total_ref[
                pl.ds(pl.multiple_of(pos * 8, 8), 8), :]
            tile = total_ref[pl.ds(pl.multiple_of(128 + 16 * (pos >> 2), 16), 16), :]
            tile = pltpu.roll(tile, (32 * (pr - pos)) & 127, 1)
            at = pl.ds(pl.multiple_of(64 + 16 * (pr >> 2), 16), 16)
            slot_ref[d, at, :] = jnp.where((lane >> 5) == (pr & 3), tile, slot_ref[d, at, :])
            rest = pltpu.roll(total_ref[192:208, :], (pr - pos) & 127, 1)
            slot_ref[d, 96:112, :] = jnp.where(
                (lane == pr) | (lane == pr + 16), rest, slot_ref[d, 96:112, :])

        return 0

    lax.fori_loop(0, LOCAL, body, 0)
    for d, out in enumerate((e0, e1, e2, e3)):
        out[...] = slot_ref[d]


def prepare_kernel(owner_ref, moment_ref, weight_ref, gene_ref,
                   source_ref, rank_ref, local_gene_ref, whiten_ref, half_ref, scale_ref,
                   weights_ref, pad_ref, system_ref, count_ref):
    x, k, g, c = (lax.axis_index(a) for a in AXES)
    me = g * 4 + c
    count_ref[0] = 0
    pad_ref[...] = jnp.zeros_like(pad_ref)
    lane1 = iota((1, WIDTH), 1)

    for source in range(4):
        count_ref[1] = 0

        def body(i, _):
            bucket = source * LOCAL + i

            @pl.when(owner_ref[bucket] == me)
            def _():
                r = count_ref[0]
                count_ref[0] = r + 1
                pr = count_ref[1]
                count_ref[1] = pr + 1
                source_ref[r] = (g - source) & 3
                rank_ref[r] = pr
                genes = gene_ref[pl.ds(bucket, 1), :]
                local_gene_ref[r] = jnp.max(genes) - me * 8
                pad_ref[pl.ds(r, 1), :] = jnp.where(genes >= 0, weight_ref[pl.ds(bucket, 1), :], 0.0)

            return 0

        lax.fori_loop(0, LOCAL, body, 0)

    weights_ref[...] = pad_ref[:16, :]
    turned = pad_ref[...].T
    pad_ref[...] = turned
    part = 2 * x + k
    mine = pad_ref[pl.ds(pl.multiple_of(part * 16, 16), 16), :]
    lane = iota((16, WIDTH), 1)
    by16 = pltpu.roll(mine, 16, 1)
    scale_ref[...] = (mine * (1.0 / 128.0) + by16 * by16 * (1.0 / SAMPLES)
                      + pltpu.roll(mine, 32, 1))

    m = moment_ref[...]
    high = pltpu.roll(m, WIDTH - 32, 1)
    low = pltpu.roll(m, WIDTH - 65, 1)
    m = jnp.concatenate([high, low], 0)
    row, lane = iota((COVS, WIDTH), 0), iota((COVS, WIDTH), 1)
    unit = jnp.where(lane == row + 64, 1.0, 0.0)
    m = jnp.where(lane <= COVS, m, 0.0) + unit
    scales = jnp.zeros((COVS, WIDTH), F32)
    for i in range(COVS):
        pivot_row = m[i:i + 1, :]
        col = jnp.sum(jnp.where(lane == i, m, 0.0), axis=1, keepdims=True)
        inv = 1.0 / col[i:i + 1, :]
        scales = jnp.where(row == i, jnp.broadcast_to(inv, (COVS, WIDTH)), scales)
        factor = jnp.where(row[:, :1] > i, col * inv, 0.0)
        m = m - factor * pivot_row
    m = m * jnp.sqrt(scales)
    linv = jnp.where(lane < COVS, pltpu.roll(m, 64, 1), 0.0)
    blocks = linv
    wide = jnp.concatenate([pltpu.roll(linv, 32 * q, 1) for q in range(4)], 0)
    whiten_ref[...] = wide
    half_col = jnp.sum(jnp.where(lane == COVS, m, 0.0), axis=1, keepdims=True)
    half_wide = jnp.concatenate([half_col] * 4, 0)
    row, lane = iota((WIDTH, WIDTH), 0), iota((WIDTH, WIDTH), 1)
    half_ref[...] = jnp.where(lane == (row >> 5), half_wide, 0.0)


def scores_kernel(source_ref, rank_ref, w0, w1, w2, w3, whiten_ref, half_ref, scale_ref,
                  out_ref, slot_ref, cross_ref):
    for d, ref in enumerate((w0, w1, w2, w3)):
        slot_ref[d] = ref[...]
    lane = iota((16, WIDTH), 1)
    rest = jnp.zeros((16, WIDTH), F32)
    for group in range(4):
        tile = jnp.zeros((16, WIDTH), F32)
        for q in range(4):
            r = group * 4 + q
            d, pr = source_ref[r], rank_ref[r]
            out_ref[r >> 1, 8 * (r & 1):8 * (r & 1) + 8, :] = slot_ref[
                d, pl.ds(pl.multiple_of(pr * 8, 8), 8), :]
            part = slot_ref[d, pl.ds(pl.multiple_of(64 + 16 * (pr >> 2), 16), 16), :]
            part = pltpu.roll(part, (32 * (q - pr)) & 127, 1)
            tile = jnp.where((lane >> 5) == q, part, tile)
            more = pltpu.roll(slot_ref[d, 96:112, :], (r - pr) & 127, 1)
            rest = jnp.where((lane == r) | (lane == r + 16), more, rest)
        cross_ref[group * 16:group * 16 + 16, :] = tile
    whitened = lax.dot_general(cross_ref[...], whiten_ref[...], (((1,), (1,)), ((), ())),
                               precision=HIGHEST, preferred_element_type=F32)
    row, col = iota((WIDTH, WIDTH), 0), iota((WIDTH, WIDTH), 1)
    ones = jnp.where(col == (row >> 5) + 16, 1.0, 0.0)
    taken = (jnp.dot(whitened, half_ref[...], precision=HIGHEST, preferred_element_type=F32)
             + jnp.dot(whitened * whitened, ones, precision=HIGHEST, preferred_element_type=F32))
    for group in range(4):
        rest = rest - pltpu.roll(taken[group * 16:group * 16 + 16], 4 * group, 1)
    scale = scale_ref[...]
    rest = jnp.where(lane < 32, rest * scale, jnp.where(lane < 48, scale, 0.0))
    for t in range(8):
        out_ref[t, 16:32, :] = whitened[(t >> 1) * 16:(t >> 1) * 16 + 16]
        out_ref[t, 32:48, :] = rest


def finish_kernel(local_gene_ref, parts_ref, weights_ref, tiles_ref, rho_ref, trace_ref):
    x, k, g, c = (lax.axis_index(a) for a in AXES)
    part = 2 * x + k
    row, lane = iota((WIDTH, WIDTH), 0), iota((WIDTH, WIDTH), 1)
    whitened = jnp.concatenate([parts_ref[t, 16:32, :] for t in range(8)], 0)
    rest = jnp.concatenate([parts_ref[t, 32:48, :] for t in range(8)], 0)
    direct = ((row < 64) & ((lane >= 64) | (row <= lane))) | ((row >= 64) & (lane >= 64) & (row > lane))
    for q in range(2):
        rank = 2 * part + q
        packed = jnp.concatenate([parts_ref[t, 8 * q:8 * q + 8, :] for t in range(8)], 0)
        full = jnp.concatenate([packed, pltpu.roll(packed, 64, 1)], 0)
        gram = jnp.where(direct, full, full.T)
        w = jnp.where((lane >> 5) == 2 * (part & 1) + q, whitened, 0.0)
        projected = lax.dot_general(w, w, (((1,), (1,)), ((), ())), precision=HIGHEST,
                                    preferred_element_type=F32)
        weight_col = jnp.sum(jnp.where(lane == 32 + rank, rest, 0.0), axis=1, keepdims=True)
        diag_col = jnp.sum(jnp.where(lane == 16 + rank, rest, 0.0), axis=1, keepdims=True)
        weight_row = weights_ref[pl.ds(rank, 1), :]
        tile = weight_col * weight_row * (gram - projected) * (1.0 / SAMPLES)
        tiles_ref[q] = jnp.where(row == lane, diag_col, tile)

    row8, lane8 = iota((8, WIDTH), 0), iota((8, WIDTH), 1)
    member = jnp.zeros((8, WIDTH), F32)
    for r in range(16):
        member = jnp.where((lane8 == r) & (row8 == local_gene_ref[r]), 1.0, member)
    squares = jnp.sum(rest * rest, axis=0, keepdims=True)
    sums = jnp.sum(rest, axis=0, keepdims=True)
    table = jnp.where(row8 == 0, squares, sums)
    nt = (((1,), (1,)), ((), ()))
    by_gene = lax.dot_general(table, member, nt, precision=HIGHEST, preferred_element_type=F32)
    traces = lax.dot_general(table, pltpu.roll(member, 16, 1), nt, precision=HIGHEST,
                             preferred_element_type=F32)
    level = iota((8, 8), 0)
    rho = jnp.zeros((8, 8), F32)
    for i, value in enumerate(RHO_GRID):
        rho = jnp.where(level == i, value, rho)
    burden = by_gene[1:2, :]
    rho_ref[...] = ((1.0 - rho) * by_gene[0:1, :] + rho * (burden * burden)) * (1.0 / WIDTH)
    trace_ref[...] = traces[1:2, :] * (1.0 / WIDTH)


def turns(d, first):
    pairs = []
    for x in range(4):
        for k in range(2):
            for g in range(4):
                for c in range(4):
                    along_x = (k == 0) == first
                    xd, cd = ((x + d) % 4, c) if along_x else (x, (c + d) % 4)
                    pairs.append((((x * 2 + k) * 4 + g) * 4 + c, ((xd * 2 + k) * 4 + g) * 4 + cd))
    return pairs


def shards(dosage, covariates, phenotype, sample_mask, variant_weight, bucket_owner, variant_gene):
    samples = dosage.shape[0]
    keep, send = products(bucket_owner, dosage, covariates, phenotype.reshape(1, samples),
                          sample_mask.reshape(1, samples))
    recv = lax.ppermute(send, "k", [(0, 1), (1, 0)])
    chunk = jax.ShapeDtypeStruct((4, CHUNK, WIDTH), F32)
    a = vmem_call(first_sum_kernel, [chunk] * 4, "first_sum", 2)(keep, recv)
    r = {d: lax.ppermute(a[d], AXES, turns(d, True)) for d in (2, 1, 3)}
    part = jax.ShapeDtypeStruct((CHUNK, WIDTH), F32)
    b = vmem_call(second_sum_kernel, [part] * 4, "second_sum", 4)(a[0], r[1], r[2], r[3])
    q = {d: lax.ppermute(b[d], AXES, turns(d, False)) for d in (2, 1, 3)}
    routed = jax.ShapeDtypeStruct((ROUTED, WIDTH), F32)
    tile16 = jax.ShapeDtypeStruct((16, WIDTH), F32)
    *e, moment = vmem_call(
        route_kernel, [routed] * 4 + [tile16], "route", 5, smem_in=1,
        scratch=[pltpu.VMEM((CHUNK, WIDTH), F32), pltpu.VMEM((4, ROUTED, WIDTH), F32),
                 pltpu.SMEM((5,), jnp.int32)],
    )(bucket_owner, b[0], q[1], q[2], q[3])
    w = {d: lax.ppermute(e[d], "g", [(i, (i + d) % 4) for i in range(4)]) for d in (2, 1, 3)}
    list16 = jax.ShapeDtypeStruct((16,), jnp.int32)
    square = jax.ShapeDtypeStruct((WIDTH, WIDTH), F32)
    source, rank, local_gene, whiten, half, scale, weights = vmem_call(
        prepare_kernel, [list16] * 3 + [square] * 2 + [tile16] * 2, "prepare", 4, smem_in=1,
        smem_out=(0, 1, 2),
        scratch=[pltpu.VMEM((WIDTH, WIDTH), F32), pltpu.VMEM((COVS, WIDTH), F32),
                 pltpu.SMEM((2,), jnp.int32)],
    )(bucket_owner, moment, variant_weight.reshape(-1, WIDTH), variant_gene.reshape(-1, WIDTH))
    (parts,) = vmem_call(
        scores_kernel, [jax.ShapeDtypeStruct((8, FINAL, WIDTH), F32)], "scores", 9, smem_in=2,
        scratch=[pltpu.VMEM((4, ROUTED, WIDTH), F32), pltpu.VMEM((64, WIDTH), F32)],
    )(source, rank, e[0], w[1], w[2], w[3], whiten, half, scale)
    parts = lax.all_to_all(parts, ("x", "k"), split_axis=0, concat_axis=0, tiled=True)
    tiles, rho, trace = vmem_call(
        finish_kernel,
        [jax.ShapeDtypeStruct((2, WIDTH, WIDTH), F32), jax.ShapeDtypeStruct((8, 8), F32),
         jax.ShapeDtypeStruct((1, 8), F32)], "finish", 3, smem_in=1,
    )(local_gene, parts, weights)
    return tiles[None], rho, trace.reshape(8)


def solution(mesh):
    grid = Mesh(mesh.devices.reshape(4, 2, 4, 4), AXES)
    rows = ("x", "k", "c")
    owners = ("g", "c")
    return jax.shard_map(
        shards,
        mesh=grid,
        in_specs=(P(rows, "g"), P(rows, None), P(rows), P(rows), P(), P(), P()),
        out_specs=(P(owners, ("x", "k"), None, None), P(None, owners), P(owners)),
        check_vma=False,
    )
```

```python
import jax
import jax.numpy as jnp
from jax import lax
from jax.experimental import pallas as pl
from jax.experimental.pallas import tpu as pltpu
from jax.sharding import Mesh, PartitionSpec as P

AXES = ("x", "k", "g", "c")
RHO_GRID = (0.0, 0.01, 0.04, 0.09, 0.16, 0.25, 0.5, 1.0)
SAMPLES = 16384
WIDTH = 128
COVS = 32
LOCAL = 64
STEP = 16
LOAD = 16
CHUNK = 208
ROUTED = 112
FINAL = 48
F32 = jnp.float32
HIGHEST = lax.Precision.HIGHEST


def params(**kwargs):
    return pltpu.CompilerParams(vmem_limit_bytes=48 * 1024 * 1024, **kwargs)


def iota(shape, dim):
    return lax.broadcasted_iota(jnp.int32, shape, dim)


def products_kernel(owner_hbm, dosage_ref, cov_hbm, pheno_hbm, mask_hbm, keep_ref, send_ref,
                    owner_ref, cov_ref, pheno_ref, mask_ref,
                    panel_ref, left_ref, packed_ref, cross_ref, rest_ref, moment_ref, count_ref,
                    sems, small_sems):
    x, k, g, c = (lax.axis_index(a) for a in AXES)
    samples = dosage_ref.shape[0]

    def fetch(i):
        at = pl.ds(pl.multiple_of(i * LOAD * WIDTH, WIDTH), LOAD * WIDTH)
        return pltpu.make_async_copy(dosage_ref.at[:, at], panel_ref.at[i], sems.at[i])

    small = [
        pltpu.make_async_copy(src, dst, small_sems.at[i])
        for i, (src, dst) in enumerate([(cov_hbm, cov_ref), (pheno_hbm, pheno_ref),
                                        (mask_hbm, mask_ref), (owner_hbm, owner_ref)])]
    for copy in small:
        copy.start()
    for i in range(LOCAL // LOAD):
        fetch(i).start()

    def place(core, xd, cd):
        first = core == 0
        d = jnp.where(first, (xd - x) & 3, (cd - c) & 3)
        j = jnp.where(first, cd, xd)
        return d, j

    rest_ref[...] = jnp.zeros_like(rest_ref)
    for i in range(4):
        count_ref[i] = 0
    for copy in small:
        copy.wait()
    cov_rows = cov_ref[...]
    pheno = jnp.concatenate([pheno_ref[i:i + 1, :] for i in range(samples // WIDTH)], 1)
    right = jnp.concatenate(
        [cov_rows, pheno, jnp.zeros((WIDTH - COVS - 1, cov_rows.shape[1]), jnp.bfloat16)], 0)
    keep = mask_ref[...].astype(F32).astype(jnp.bfloat16)
    masked = right[:48] * keep
    left_ref[...] = masked
    m = lax.dot_general(masked[:COVS], right, (((1,), (1,)), ((), ())),
                        preferred_element_type=F32)
    moment_ref[...] = pltpu.roll(m[:16], 32, 1) + pltpu.roll(m[16:32], 65, 1)

    keep_row = mask_ref[...].astype(F32).astype(jnp.bfloat16)
    row, lane = iota((64, WIDTH), 0), iota((64, WIDTH), 1)
    take_low = (lane < 64) & (row > lane)
    eye = iota((WIDTH, WIDTH), 0) == iota((WIDTH, WIDTH), 1)
    def run(step, _):
        for pair in range(STEP // 2):
            load = step * (STEP // LOAD) + pair * 2 // LOAD
            if pair * 2 % LOAD == 0:
                fetch(load).wait()
            lo = pair * 256 % (LOAD * WIDTH)
            panel = panel_ref[load, :, lo:lo + 256]
            left = jnp.concatenate([panel.T * keep_row, left_ref[...]], 0)
            out = jnp.dot(left, panel, preferred_element_type=F32)
            for half in range(2):
                lo = half * WIDTH
                block = out[lo:lo + WIDTH, lo:lo + WIDTH]
                bucket = step * STEP + pair * 2 + half
                cd = owner_ref[g * LOCAL + bucket] & 3
                pos = count_ref[cd]
                count_ref[cd] = pos + 1
                slot = pair * 2 + half
                packed_ref[slot] = jnp.where(take_low, pltpu.roll(block[64:], 64, 1), block[:64])
                rows = pl.ds(pl.multiple_of(pos * 8, 8), 8)
                for xd in range(4):
                    d, j = place(k, xd, cd)
                    keep_ref[d, j, rows, :] = packed_ref[
                        slot, pl.ds(pl.multiple_of((2 * xd + k) * 8, 8), 8), :]
                    d, j = place(1 - k, xd, cd)
                    send_ref[d, j, rows, :] = packed_ref[
                        slot, pl.ds(pl.multiple_of((2 * xd + 1 - k) * 8, 8), 8), :]
                cross_ref[cd, pl.ds(pl.multiple_of(pos * COVS, 8), COVS), :] = out[
                    256:256 + COVS, lo:lo + WIDTH]
                rest_ref[cd, pl.ds(pos, 1), :] = out[256 + COVS:257 + COVS, lo:lo + WIDTH]
                rest_ref[cd, pl.ds(pos + 16, 1), :] = jnp.sum(
                    jnp.where(eye, block, 0.0), axis=0, keepdims=True)
        return 0

    lax.fori_loop(0, LOCAL // STEP, run, 0)

    for cd in range(4):
        for q in range(5):
            if q < 4:
                turned = cross_ref[cd, q * WIDTH:(q + 1) * WIDTH, :].T
            else:
                turned = rest_ref[cd].T
            for t in range(8):
                tile = turned[16 * t:16 * t + 16]
                if q == 4:
                    tile = tile + moment_ref[...]
                rows = slice(128 + 16 * q, 144 + 16 * q)
                d, j = place(t & 1, t >> 1, cd)

                @pl.when(k == (t & 1))
                def _():
                    keep_ref[d, j, rows, :] = tile

                @pl.when(k != (t & 1))
                def _():
                    send_ref[d, j, rows, :] = tile


def products(owner, dosage, cov, pheno, mask):
    samples = dosage.shape[0]
    out = jax.ShapeDtypeStruct((4, 4, CHUNK, WIDTH), F32)
    vmem = pl.BlockSpec(memory_space=pltpu.VMEM)
    return pl.pallas_call(
        products_kernel,
        out_shape=(out, out),
        in_specs=[pl.BlockSpec(memory_space=pltpu.HBM)] * 5,
        out_specs=(vmem, vmem),
        scratch_shapes=[
            pltpu.SMEM(owner.shape, jnp.int32),
            pltpu.VMEM(cov.shape, jnp.bfloat16),
            pltpu.VMEM(pheno.shape, jnp.bfloat16),
            pltpu.VMEM(mask.shape, jnp.int32),
            pltpu.VMEM((LOCAL // LOAD, samples, LOAD * WIDTH), jnp.bfloat16),
            pltpu.VMEM((48, samples), jnp.bfloat16),
            pltpu.VMEM((STEP, 64, WIDTH), F32),
            pltpu.VMEM((4, 16 * COVS, WIDTH), F32),
            pltpu.VMEM((4, WIDTH, WIDTH), F32),
            pltpu.VMEM((16, WIDTH), F32),
            pltpu.SMEM((4,), jnp.int32),
            pltpu.SemaphoreType.DMA((LOCAL // LOAD,)),
            pltpu.SemaphoreType.DMA((4,)),
        ],
        compiler_params=params(),
        name="products",
    )(*[pltpu.with_memory_space_constraint(a, pltpu.HBM)
        for a in (owner, dosage, cov, pheno, mask)])


def first_sum_kernel(keep_ref, recv_ref, *outs):
    for d in range(4):
        outs[d][...] = keep_ref[d] + recv_ref[d]


def second_sum_kernel(a0, r2, r1, r3, _, *outs):
    x, k, g, c = (lax.axis_index(a) for a in AXES)
    base = jnp.where(k == 0, c, x)
    for d in range(4):
        j = (base + d) & 3
        outs[d][...] = (a0[j] + r1[j]) + (r2[j] + r3[j])


def vmem_call(kernel, shapes, name, n_in, scratch=(), smem_in=0, smem_out=(), any_in=0):
    specs = [pl.BlockSpec(memory_space=pltpu.SMEM)] * smem_in + [
        pl.BlockSpec(memory_space=pltpu.VMEM)] * (n_in - smem_in - any_in) + [
        pl.BlockSpec(memory_space=pl.ANY)] * any_in
    return pl.pallas_call(
        kernel,
        out_shape=tuple(shapes),
        in_specs=specs,
        out_specs=tuple(
            pl.BlockSpec(memory_space=pltpu.SMEM if i in smem_out else pltpu.VMEM)
            for i in range(len(shapes))),
        scratch_shapes=scratch,
        compiler_params=params(),
        name=name,
    )


def route_kernel(turn_ref, slot_at_ref, b0, q2, q1, q3, e0, e1, e2, e3, moment_ref, total_ref,
                 slot_ref):
    total_ref[...] = (b0[...] + q1[...]) + (q2[...] + q3[...])
    rest = total_ref[192:208, :]
    moment_ref[...] = rest
    slot_ref[...] = jnp.zeros_like(slot_ref)
    lane = iota((16, WIDTH), 1)
    for pos in range(16):
        d, pr = turn_ref[pos], slot_at_ref[pos]
        slot_ref[d, pl.ds(pl.multiple_of(pr * 8, 8), 8), :] = total_ref[8 * pos:8 * pos + 8, :]
        tile = total_ref[128 + 16 * (pos >> 2):144 + 16 * (pos >> 2), :]
        tile = pltpu.roll(tile, (32 * (pr - pos)) & 127, 1)
        at = pl.ds(pl.multiple_of(64 + 16 * (pr >> 2), 16), 16)
        slot_ref[d, at, :] = jnp.where((lane >> 5) == (pr & 3), tile, slot_ref[d, at, :])
        slot_ref[d, 96:112, :] = jnp.where(
            (lane == pr) | (lane == pr + 16), pltpu.roll(rest, (pr - pos) & 127, 1),
            slot_ref[d, 96:112, :])
    for d, out in enumerate((e0, e1, e2, e3)):
        out[...] = slot_ref[d]


def layout_kernel(owner_ref, weight_ref, gene_ref, _, turn_ref, slot_at_ref, source_ref, rank_ref,
                  local_gene_ref, scale_ref, weights_ref, pad_ref, count_ref):
    x, k, g, c = (lax.axis_index(a) for a in AXES)
    me = g * 4 + c
    for i in range(6):
        count_ref[i] = 0
    pad_ref[...] = jnp.zeros_like(pad_ref)

    def outgoing(i, _):
        owner = owner_ref[g * LOCAL + i]

        @pl.when((owner & 3) == c)
        def _():
            pos = count_ref[4]
            count_ref[4] = pos + 1
            gd = owner >> 2
            pr = count_ref[gd]
            count_ref[gd] = pr + 1
            turn_ref[pos] = (gd - g) & 3
            slot_at_ref[pos] = pr

        return 0

    lax.fori_loop(0, LOCAL, outgoing, 0)
    count_ref[4] = 0

    for source in range(4):
        count_ref[5] = 0

        def owned(i, _):
            bucket = source * LOCAL + i

            @pl.when(owner_ref[bucket] == me)
            def _():
                r = count_ref[4]
                count_ref[4] = r + 1
                pr = count_ref[5]
                count_ref[5] = pr + 1
                source_ref[r] = (g - source) & 3
                rank_ref[r] = pr
                genes = gene_ref[pl.ds(bucket, 1), :]
                local_gene_ref[r] = jnp.max(genes) - me * 8
                pad_ref[pl.ds(r, 1), :] = jnp.where(
                    genes >= 0, weight_ref[pl.ds(bucket, 1), :], 0.0)

            return 0

        lax.fori_loop(0, LOCAL, owned, 0)

    weights_ref[...] = pad_ref[:16, :]
    pad_ref[...] = pad_ref[...].T
    mine = pad_ref[pl.ds(pl.multiple_of((2 * x + k) * 16, 16), 16), :]
    by16 = pltpu.roll(mine, 16, 1)
    scale_ref[...] = (mine * (1.0 / 128.0) + by16 * by16 * (1.0 / SAMPLES)
                      + pltpu.roll(mine, 32, 1))


def solve_kernel(moment_ref, whiten_ref, half_ref):
    m = moment_ref[...]
    m = jnp.concatenate([pltpu.roll(m, WIDTH - 32, 1), pltpu.roll(m, WIDTH - 65, 1)], 0)
    row, lane = iota((COVS, WIDTH), 0), iota((COVS, WIDTH), 1)
    m = jnp.where(lane <= COVS, m, jnp.where(lane == row + 64, 1.0, 0.0))
    scales = jnp.zeros((COVS, WIDTH), F32)
    for i in range(COVS):
        col = jnp.broadcast_to(m[:, i:i + 1], m.shape)
        inv = 1.0 / col[i:i + 1, :]
        scales = jnp.where(row == i, inv, scales)
        m = m - jnp.where(row > i, col * inv, 0.0) * m[i:i + 1, :]
    m = m * jnp.sqrt(scales)
    inverse = jnp.where(lane < COVS, pltpu.roll(m, 64, 1), 0.0)
    whiten_ref[...] = jnp.concatenate(
        [inverse] + [pltpu.roll(inverse, 32 * q, 1) for q in range(1, 4)], 0)
    half = jnp.concatenate([jnp.broadcast_to(m[:, COVS:COVS + 1], m.shape)] * 4, 0)
    row, lane = iota((WIDTH, WIDTH), 0), iota((WIDTH, WIDTH), 1)
    half_ref[...] = jnp.where(lane == (row >> 5), half, 0.0)


def scores_kernel(source_ref, rank_ref, w0, w2, w1, w3, whiten_ref, half_ref, scale_ref,
                  out_ref, slot_ref, cross_ref):
    for d, ref in enumerate((w0, w1, w2, w3)):
        slot_ref[d] = ref[...]
    lane = iota((16, WIDTH), 1)
    rest = jnp.zeros((16, WIDTH), F32)
    for group in range(4):
        tile = jnp.zeros((16, WIDTH), F32)
        for q in range(4):
            r = group * 4 + q
            d, pr = source_ref[r], rank_ref[r]
            out_ref[r >> 1, 8 * (r & 1):8 * (r & 1) + 8, :] = slot_ref[
                d, pl.ds(pl.multiple_of(pr * 8, 8), 8), :]
            part = slot_ref[d, pl.ds(pl.multiple_of(64 + 16 * (pr >> 2), 16), 16), :]
            part = pltpu.roll(part, (32 * (q - pr)) & 127, 1)
            tile = jnp.where((lane >> 5) == q, part, tile)
            more = pltpu.roll(slot_ref[d, 96:112, :], (r - pr) & 127, 1)
            rest = jnp.where((lane == r) | (lane == r + 16), more, rest)
        cross_ref[group * 16:group * 16 + 16, :] = tile
    whitened = lax.dot_general(cross_ref[...], whiten_ref[...], (((1,), (1,)), ((), ())),
                               precision=HIGHEST, preferred_element_type=F32)
    row, col = iota((WIDTH, WIDTH), 0), iota((WIDTH, WIDTH), 1)
    ones = jnp.where(col == (row >> 5) + 16, 1.0, 0.0)
    taken = (jnp.dot(whitened, half_ref[...], precision=HIGHEST, preferred_element_type=F32)
             + jnp.dot(whitened * whitened, ones, precision=HIGHEST, preferred_element_type=F32))
    for group in range(4):
        rest = rest - pltpu.roll(taken[group * 16:group * 16 + 16], 4 * group, 1)
    scale = scale_ref[...]
    rest = jnp.where(lane < 32, rest * scale, jnp.where(lane < 48, scale, 0.0))
    for t in range(8):
        out_ref[t, 16:32, :] = whitened[(t >> 1) * 16:(t >> 1) * 16 + 16]
        out_ref[t, 32:48, :] = rest


def finish_kernel(local_gene_ref, parts_ref, weights_ref, tiles_ref, rho_ref, trace_ref):
    x, k, g, c = (lax.axis_index(a) for a in AXES)
    part = 2 * x + k
    row, lane = iota((WIDTH, WIDTH), 0), iota((WIDTH, WIDTH), 1)
    whitened = jnp.concatenate([parts_ref[t, 16:32, :] for t in range(8)], 0)
    rest = jnp.concatenate([parts_ref[t, 32:48, :] for t in range(8)], 0)
    direct = ((row < 64) & ((lane >= 64) | (row <= lane))) | ((row >= 64) & (lane >= 64) & (row > lane))
    for q in range(2):
        rank = 2 * part + q
        packed = jnp.concatenate([parts_ref[t, 8 * q:8 * q + 8, :] for t in range(8)], 0)
        full = jnp.concatenate([packed, pltpu.roll(packed, 64, 1)], 0)
        gram = jnp.where(direct, full, full.T)
        w = jnp.where((lane >> 5) == 2 * (part & 1) + q, whitened, 0.0)
        projected = lax.dot_general(w, w, (((1,), (1,)), ((), ())), precision=HIGHEST,
                                    preferred_element_type=F32)
        weight_col = jnp.sum(jnp.where(lane == 32 + rank, rest, 0.0), axis=1, keepdims=True)
        diag_col = jnp.sum(jnp.where(lane == 16 + rank, rest, 0.0), axis=1, keepdims=True)
        weight_row = weights_ref[pl.ds(rank, 1), :]
        tile = weight_col * weight_row * (gram - projected) * (1.0 / SAMPLES)
        tiles_ref[q] = jnp.where(row == lane, diag_col, tile)

    row8, lane8 = iota((8, WIDTH), 0), iota((8, WIDTH), 1)
    member = jnp.zeros((8, WIDTH), F32)
    for r in range(16):
        member = jnp.where((lane8 == r) & (row8 == local_gene_ref[r]), 1.0, member)
    squares = jnp.sum(rest * rest, axis=0, keepdims=True)
    sums = jnp.sum(rest, axis=0, keepdims=True)
    table = jnp.where(row8 == 0, squares, sums)
    nt = (((1,), (1,)), ((), ()))
    by_gene = lax.dot_general(table, member, nt, precision=HIGHEST, preferred_element_type=F32)
    traces = lax.dot_general(table, pltpu.roll(member, 16, 1), nt, precision=HIGHEST,
                             preferred_element_type=F32)
    level = iota((8, 8), 0)
    rho = jnp.zeros((8, 8), F32)
    for i, value in enumerate(RHO_GRID):
        rho = jnp.where(level == i, value, rho)
    burden = by_gene[1:2, :]
    rho_ref[...] = ((1.0 - rho) * by_gene[0:1, :] + rho * (burden * burden)) * (1.0 / WIDTH)
    trace_ref[...] = traces[1:2, :] * (1.0 / WIDTH)


def turns(d, first):
    pairs = []
    for x in range(4):
        for k in range(2):
            for g in range(4):
                for c in range(4):
                    along_x = (k == 0) == first
                    xd, cd = ((x + d) % 4, c) if along_x else (x, (c + d) % 4)
                    pairs.append((((x * 2 + k) * 4 + g) * 4 + c, ((xd * 2 + k) * 4 + g) * 4 + cd))
    return pairs


def shards(dosage, covariates, phenotype, sample_mask, variant_weight, bucket_owner, variant_gene):
    samples = dosage.shape[0]
    keep, send = products(bucket_owner, dosage, covariates.T, phenotype.reshape(-1, WIDTH),
                          sample_mask.reshape(1, samples))
    recv = lax.ppermute(send, "k", [(0, 1), (1, 0)])
    chunk = jax.ShapeDtypeStruct((4, CHUNK, WIDTH), F32)
    a = vmem_call(first_sum_kernel, [chunk] * 4, "first_sum", 2)(keep, recv)
    r = {d: lax.ppermute(a[d], AXES, turns(d, True)) for d in (2, 1, 3)}
    list16 = jax.ShapeDtypeStruct((16,), jnp.int32)
    square = jax.ShapeDtypeStruct((WIDTH, WIDTH), F32)
    tile16 = jax.ShapeDtypeStruct((16, WIDTH), F32)
    turn, slot_at, source, rank, local_gene, scale, weights = vmem_call(
        layout_kernel, [list16] * 5 + [tile16] * 2, "layout", 4, smem_in=1,
        smem_out=(0, 1, 2, 3, 4), any_in=1,
        scratch=[pltpu.VMEM((WIDTH, WIDTH), F32), pltpu.SMEM((6,), jnp.int32)],
    )(bucket_owner, variant_weight.reshape(-1, WIDTH), variant_gene.reshape(-1, WIDTH), a[0])
    part = jax.ShapeDtypeStruct((CHUNK, WIDTH), F32)
    b = vmem_call(second_sum_kernel, [part] * 4, "second_sum", 5, any_in=1)(
        a[0], r[2], r[1], r[3], weights)
    q = {d: lax.ppermute(b[d], AXES, turns(d, False)) for d in (2, 1, 3)}
    routed = jax.ShapeDtypeStruct((ROUTED, WIDTH), F32)
    *e, moment = vmem_call(
        route_kernel, [routed] * 4 + [tile16], "route", 6, smem_in=2,
        scratch=[pltpu.VMEM((CHUNK, WIDTH), F32), pltpu.VMEM((4, ROUTED, WIDTH), F32)],
    )(turn, slot_at, b[0], q[2], q[1], q[3])
    w = {d: lax.ppermute(e[d], "g", [(i, (i + d) % 4) for i in range(4)]) for d in (2, 1, 3)}
    whiten, half = vmem_call(solve_kernel, [square] * 2, "solve", 1)(moment)
    (parts,) = vmem_call(
        scores_kernel, [jax.ShapeDtypeStruct((8, FINAL, WIDTH), F32)], "scores", 9, smem_in=2,
        scratch=[pltpu.VMEM((4, ROUTED, WIDTH), F32), pltpu.VMEM((64, WIDTH), F32)],
    )(source, rank, e[0], w[2], w[1], w[3], whiten, half, scale)
    parts = lax.all_to_all(parts, ("x", "k"), split_axis=0, concat_axis=0, tiled=True)
    tiles, rho, trace = vmem_call(
        finish_kernel,
        [jax.ShapeDtypeStruct((2, WIDTH, WIDTH), F32), jax.ShapeDtypeStruct((8, 8), F32),
         jax.ShapeDtypeStruct((1, 8), F32)], "finish", 3, smem_in=1,
    )(local_gene, parts, weights)
    return tiles[None], rho, trace.reshape(8)


def solution(mesh):
    grid = Mesh(mesh.devices.reshape(4, 2, 4, 4), AXES)
    rows = ("x", "k", "c")
    owners = ("g", "c")
    return jax.shard_map(
        shards,
        mesh=grid,
        in_specs=(P(rows, "g"), P(rows, None), P(rows), P(rows), P(), P(), P()),
        out_specs=(P(owners, ("x", "k"), None, None), P(None, owners), P(owners)),
        check_vma=False,
    )
```

```python
import jax
import jax.numpy as jnp
from jax import lax
from jax.experimental import pallas as pl
from jax.experimental.pallas import tpu as pltpu
from jax.sharding import Mesh, PartitionSpec as P

AXES = ("x", "k", "g", "c")
RHO_GRID = (0.0, 0.01, 0.04, 0.09, 0.16, 0.25, 0.5, 1.0)
SAMPLES = 16384
WIDTH = 128
COVS = 32
LOCAL = 64
STEP = 16
LOAD = 16
GRAM = 128
CROSS = 80
CHUNK = GRAM + CROSS
ROUTED = 112
FINAL = 48
F32 = jnp.float32
HIGHEST = lax.Precision.HIGHEST


def params(**kwargs):
    return pltpu.CompilerParams(vmem_limit_bytes=48 * 1024 * 1024, **kwargs)


def iota(shape, dim):
    return lax.broadcasted_iota(jnp.int32, shape, dim)


def placed(core, xd, cd):
    x, k, g, c = (lax.axis_index(a) for a in AXES)
    first = core == 0
    return jnp.where(first, (xd - x) & 3, (cd - c) & 3), jnp.where(first, cd, xd)


def products_kernel(owner_hbm, dosage_ref, cov_hbm, pheno_hbm, mask_hbm, keep_ref, send_ref,
                    cross_ref, rest_ref, moment_ref, owner_ref, cov_ref, pheno_ref, mask_ref,
                    panel_ref, left_ref, packed_ref, count_ref, sems, small_sems):
    x, k, g, c = (lax.axis_index(a) for a in AXES)
    samples = dosage_ref.shape[0]

    def fetch(i):
        at = pl.ds(pl.multiple_of(i * LOAD * WIDTH, WIDTH), LOAD * WIDTH)
        return pltpu.make_async_copy(dosage_ref.at[:, at], panel_ref.at[i], sems.at[i])

    small = [
        pltpu.make_async_copy(src, dst, small_sems.at[i])
        for i, (src, dst) in enumerate([(cov_hbm, cov_ref), (pheno_hbm, pheno_ref),
                                        (mask_hbm, mask_ref), (owner_hbm, owner_ref)])]
    for copy in small:
        copy.start()
    for i in range(LOCAL // LOAD):
        fetch(i).start()

    rest_ref[...] = jnp.zeros_like(rest_ref)
    for i in range(4):
        count_ref[i] = 0
    for copy in small:
        copy.wait()
    cov_rows = cov_ref[...]
    pheno = jnp.concatenate([pheno_ref[i:i + 1, :] for i in range(samples // WIDTH)], 1)
    right = jnp.concatenate(
        [cov_rows, pheno, jnp.zeros((WIDTH - COVS - 1, cov_rows.shape[1]), jnp.bfloat16)], 0)
    keep = mask_ref[...].astype(F32).astype(jnp.bfloat16)
    masked = right[:48] * keep
    left_ref[...] = masked
    m = lax.dot_general(masked[:COVS], right, (((1,), (1,)), ((), ())),
                        preferred_element_type=F32)
    moment_ref[...] = pltpu.roll(m[:16], 32, 1) + pltpu.roll(m[16:32], 65, 1)

    keep_row = mask_ref[...].astype(F32).astype(jnp.bfloat16)
    row, lane = iota((64, WIDTH), 0), iota((64, WIDTH), 1)
    take_low = (lane < 64) & (row > lane)
    eye = iota((WIDTH, WIDTH), 0) == iota((WIDTH, WIDTH), 1)
    def run(step, _):
        for pair in range(STEP // 2):
            load = step * (STEP // LOAD) + pair * 2 // LOAD
            if pair * 2 % LOAD == 0:
                fetch(load).wait()
            lo = pair * 256 % (LOAD * WIDTH)
            panel = panel_ref[load, :, lo:lo + 256]
            left = jnp.concatenate([panel.T * keep_row, left_ref[...]], 0)
            out = jnp.dot(left, panel, preferred_element_type=F32)
            for half in range(2):
                lo = half * WIDTH
                block = out[lo:lo + WIDTH, lo:lo + WIDTH]
                bucket = step * STEP + pair * 2 + half
                cd = owner_ref[g * LOCAL + bucket] & 3
                pos = count_ref[cd]
                count_ref[cd] = pos + 1
                slot = pair * 2 + half
                packed_ref[slot] = jnp.where(take_low, pltpu.roll(block[64:], 64, 1), block[:64])
                rows = pl.ds(pl.multiple_of(pos * 8, 8), 8)
                for xd in range(4):
                    d, j = placed(k, xd, cd)
                    keep_ref[d, j, rows, :] = packed_ref[
                        slot, pl.ds(pl.multiple_of((2 * xd + k) * 8, 8), 8), :]
                    d, j = placed(1 - k, xd, cd)
                    send_ref[d, j, rows, :] = packed_ref[
                        slot, pl.ds(pl.multiple_of((2 * xd + 1 - k) * 8, 8), 8), :]
                cross_ref[cd, pl.ds(pl.multiple_of(pos * COVS, 8), COVS), :] = out[
                    256:256 + COVS, lo:lo + WIDTH]
                rest_ref[cd, pl.ds(pos, 1), :] = out[256 + COVS:257 + COVS, lo:lo + WIDTH]
                rest_ref[cd, pl.ds(pos + 16, 1), :] = jnp.sum(
                    jnp.where(eye, block, 0.0), axis=0, keepdims=True)
        return 0

    lax.fori_loop(0, LOCAL // STEP, run, 0)


def cross_kernel(cross_ref, rest_ref, moment_ref, keep_ref, send_ref, turned_ref):
    k = lax.axis_index("k")
    for cd in range(4):
        for q in range(5):
            slot = cd * 5 + q
            if q < 4:
                turned_ref[slot] = cross_ref[cd, q * WIDTH:(q + 1) * WIDTH, :].T
            else:
                moment = moment_ref[...]
                turned_ref[slot] = rest_ref[cd].T + jnp.concatenate([moment] * 8, 0)
            for xd in range(4):
                for core, ref in ((k, keep_ref), (1 - k, send_ref)):
                    d, j = placed(core, xd, cd)
                    at = pl.ds(pl.multiple_of((2 * xd + core) * 16, 16), 16)
                    ref[d, j, 16 * q:16 * q + 16, :] = turned_ref[slot, at, :]


def products(owner, dosage, cov, pheno, mask):
    samples = dosage.shape[0]
    vmem = pl.BlockSpec(memory_space=pltpu.VMEM)
    shapes = [(4, 4, GRAM, WIDTH)] * 2 + [(4, 16 * COVS, WIDTH), (4, WIDTH, WIDTH), (16, WIDTH)]
    return pl.pallas_call(
        products_kernel,
        out_shape=tuple(jax.ShapeDtypeStruct(shape, F32) for shape in shapes),
        in_specs=[pl.BlockSpec(memory_space=pltpu.HBM)] * 5,
        out_specs=(vmem,) * 5,
        scratch_shapes=[
            pltpu.SMEM(owner.shape, jnp.int32),
            pltpu.VMEM(cov.shape, jnp.bfloat16),
            pltpu.VMEM(pheno.shape, jnp.bfloat16),
            pltpu.VMEM(mask.shape, jnp.int32),
            pltpu.VMEM((LOCAL // LOAD, samples, LOAD * WIDTH), jnp.bfloat16),
            pltpu.VMEM((48, samples), jnp.bfloat16),
            pltpu.VMEM((STEP, 64, WIDTH), F32),
            pltpu.SMEM((4,), jnp.int32),
            pltpu.SemaphoreType.DMA((LOCAL // LOAD,)),
            pltpu.SemaphoreType.DMA((4,)),
        ],
        compiler_params=params(),
        name="products",
    )(*[pltpu.with_memory_space_constraint(a, pltpu.HBM)
        for a in (owner, dosage, cov, pheno, mask)])


def first_sum_kernel(keep_ref, recv_ref, *outs):
    for d in range(4):
        outs[d][...] = keep_ref[d] + recv_ref[d]


def second_sum_kernel(a0, a2, a1, a3, c0, c2, c1, c3, _, *outs):
    x, k, g, c = (lax.axis_index(a) for a in AXES)
    base = jnp.where(k == 0, c, x)
    for d in range(4):
        j = (base + d) & 3
        outs[d][:GRAM] = (a0[j] + a1[j]) + (a2[j] + a3[j])
        outs[d][GRAM:] = (c0[j] + c1[j]) + (c2[j] + c3[j])


def vmem_call(kernel, shapes, name, n_in, scratch=(), smem_in=0, smem_out=(), any_in=0):
    specs = [pl.BlockSpec(memory_space=pltpu.SMEM)] * smem_in + [
        pl.BlockSpec(memory_space=pltpu.VMEM)] * (n_in - smem_in - any_in) + [
        pl.BlockSpec(memory_space=pl.ANY)] * any_in
    return pl.pallas_call(
        kernel,
        out_shape=tuple(shapes),
        in_specs=specs,
        out_specs=tuple(
            pl.BlockSpec(memory_space=pltpu.SMEM if i in smem_out else pltpu.VMEM)
            for i in range(len(shapes))),
        scratch_shapes=scratch,
        compiler_params=params(),
        name=name,
    )


def route_kernel(turn_ref, slot_at_ref, b0, q2, q1, q3, e0, e1, e2, e3, moment_ref, total_ref,
                 slot_ref):
    total_ref[...] = (b0[...] + q1[...]) + (q2[...] + q3[...])
    rest = total_ref[192:208, :]
    moment_ref[...] = rest
    slot_ref[...] = jnp.zeros_like(slot_ref)
    lane = iota((16, WIDTH), 1)
    for pos in range(16):
        d, pr = turn_ref[pos], slot_at_ref[pos]
        slot_ref[d, pl.ds(pl.multiple_of(pr * 8, 8), 8), :] = total_ref[8 * pos:8 * pos + 8, :]
        tile = total_ref[128 + 16 * (pos >> 2):144 + 16 * (pos >> 2), :]
        tile = pltpu.roll(tile, (32 * (pr - pos)) & 127, 1)
        at = pl.ds(pl.multiple_of(64 + 16 * (pr >> 2), 16), 16)
        slot_ref[d, at, :] = jnp.where((lane >> 5) == (pr & 3), tile, slot_ref[d, at, :])
        slot_ref[d, 96:112, :] = jnp.where(
            (lane == pr) | (lane == pr + 16), pltpu.roll(rest, (pr - pos) & 127, 1),
            slot_ref[d, 96:112, :])
    for d, out in enumerate((e0, e1, e2, e3)):
        out[...] = slot_ref[d]


def layout_kernel(owner_ref, weight_ref, gene_ref, _, turn_ref, slot_at_ref, source_ref, rank_ref,
                  genes_ref, scale_ref, weights_ref, pad_ref, label_ref, list_ref, count_ref):
    x, k, g, c = (lax.axis_index(a) for a in AXES)
    me = g * 4 + c
    for i in range(4):
        count_ref[i] = 0
    pad_ref[...] = jnp.zeros_like(pad_ref)

    def scan(start, count, wanted, list_ref, value):
        def body(i, end):
            for u in range(8):
                bucket = start + i * 8 + u
                owner = owner_ref[bucket]
                list_ref[end] = value(bucket, owner)
                end = end + wanted(owner).astype(jnp.int32)
            return end

        lax.fori_loop(0, count // 8, body, 0)

    scan(g * LOCAL, LOCAL, lambda owner: (owner & 3) == c, list_ref, lambda b, owner: owner >> 2)
    for pos in range(16):
        gd = list_ref[pos]
        pr = count_ref[gd]
        count_ref[gd] = pr + 1
        turn_ref[pos] = (gd - g) & 3
        slot_at_ref[pos] = pr
    scan(0, 4 * LOCAL, lambda owner: owner == me, list_ref, lambda b, owner: b)
    last, pr = -1, 0
    for r in range(16):
        bucket = list_ref[r]
        source = bucket >> 6
        pr = jnp.where(source == last, pr + 1, 0)
        last = source
        source_ref[r] = (g - source) & 3
        rank_ref[r] = pr
        genes = gene_ref[pl.ds(bucket, 1), :]
        pad_ref[r:r + 1, :] = jnp.where(genes >= 0, weight_ref[pl.ds(bucket, 1), :], 0.0)
        label_ref[r:r + 1, :] = genes
    labels = jnp.max(label_ref[...], axis=1, keepdims=True)
    genes_ref[...] = jnp.broadcast_to(labels - me * 8, genes_ref.shape)

    weights_ref[...] = pad_ref[:16, :]
    pad_ref[...] = pad_ref[...].T
    mine = pad_ref[pl.ds(pl.multiple_of((2 * x + k) * 16, 16), 16), :]
    by16 = pltpu.roll(mine, 16, 1)
    scale_ref[...] = (mine * (1.0 / 128.0) + by16 * by16 * (1.0 / SAMPLES)
                      + pltpu.roll(mine, 32, 1))


def solve_kernel(moment_ref, whiten_ref, half_ref):
    m = moment_ref[...]
    m = jnp.concatenate([pltpu.roll(m, WIDTH - 32, 1), pltpu.roll(m, WIDTH - 65, 1)], 0)
    row, lane = iota((COVS, WIDTH), 0), iota((COVS, WIDTH), 1)
    m = jnp.where(lane <= COVS, m, jnp.where(lane == row + 64, 1.0, 0.0))
    first = jnp.zeros((COVS, WIDTH), F32)
    mixed = jnp.zeros((COVS, WIDTH), F32)
    second = jnp.ones((COVS, WIDTH), F32)
    for i in range(0, COVS, 2):
        col0 = jnp.broadcast_to(m[:, i:i + 1], m.shape)
        col1 = jnp.broadcast_to(m[:, i + 1:i + 2], m.shape)
        a, b, d = col0[i:i + 1, :], col0[i + 1:i + 2, :], col1[i + 1:i + 2, :]
        inv = 1.0 / (a * d - b * b)
        below = row > i + 1
        first = jnp.where(row >= i, a, first)
        mixed = jnp.where(row == i + 1, b, mixed)
        second = jnp.where(row == i, a, jnp.where(row == i + 1, d, second))
        m = (m - jnp.where(below, (col0 * d - col1 * b) * inv, 0.0) * m[i:i + 1, :]
             - jnp.where(below, (col1 * a - col0 * b) * inv, 0.0) * m[i + 1:i + 2, :])
    ratio = mixed / first
    m = (m - ratio * pltpu.roll(m, 1, 0)) * lax.rsqrt(second - mixed * ratio)
    inverse = jnp.where(lane < COVS, pltpu.roll(m, 64, 1), 0.0)
    whiten_ref[...] = jnp.concatenate(
        [inverse] + [pltpu.roll(inverse, 32 * q, 1) for q in range(1, 4)], 0)
    half = jnp.concatenate([jnp.broadcast_to(m[:, COVS:COVS + 1], m.shape)] * 4, 0)
    row, lane = iota((WIDTH, WIDTH), 0), iota((WIDTH, WIDTH), 1)
    half_ref[...] = jnp.where(lane == (row >> 5), half, 0.0)


def scores_kernel(source_ref, rank_ref, w0, w2, w1, w3, whiten_ref, half_ref, scale_ref,
                  mine_ref, other_ref, slot_ref, cross_ref):
    x, k = lax.axis_index("x"), lax.axis_index("k")
    for d, ref in enumerate((w0, w1, w2, w3)):
        slot_ref[d] = ref[...]
    lane = iota((16, WIDTH), 1)
    rest = jnp.zeros((16, WIDTH), F32)
    for group in range(4):
        tile = jnp.zeros((16, WIDTH), F32)
        for q in range(4):
            r = group * 4 + q
            d, pr = source_ref[r], rank_ref[r]
            part = slot_ref[d, pl.ds(pl.multiple_of(64 + 16 * (pr >> 2), 16), 16), :]
            part = pltpu.roll(part, (32 * (q - pr)) & 127, 1)
            tile = jnp.where((lane >> 5) == q, part, tile)
            more = pltpu.roll(slot_ref[d, 96:112, :], (r - pr) & 127, 1)
            rest = jnp.where((lane == r) | (lane == r + 16), more, rest)
        cross_ref[group * 16:group * 16 + 16, :] = tile
    whitened = lax.dot_general(cross_ref[...], whiten_ref[...], (((1,), (1,)), ((), ())),
                               precision=HIGHEST, preferred_element_type=F32)
    row, col = iota((WIDTH, WIDTH), 0), iota((WIDTH, WIDTH), 1)
    ones = jnp.where(col == (row >> 5) + 16, 1.0, 0.0)
    taken = (jnp.dot(whitened, half_ref[...], precision=HIGHEST, preferred_element_type=F32)
             + jnp.dot(whitened * whitened, ones, precision=HIGHEST, preferred_element_type=F32))
    for group in range(4):
        rest = rest - pltpu.roll(taken[group * 16:group * 16 + 16], 4 * group, 1)
    scale = scale_ref[...]
    rest = jnp.where(lane < 32, rest * scale, jnp.where(lane < 48, scale, 0.0))
    cross_ref[...] = whitened
    for d in range(4):
        xd = (x + d) & 3
        for core, ref in ((k, mine_ref), (1 - k, other_ref)):
            for q in range(2):
                r = 4 * xd + 2 * core + q
                ref[d, 8 * q:8 * q + 8, :] = slot_ref[
                    source_ref[r], pl.ds(pl.multiple_of(rank_ref[r] * 8, 8), 8), :]
            ref[d, 16:32, :] = cross_ref[pl.ds(pl.multiple_of(16 * xd, 16), 16), :]
            ref[d, 32:48, :] = rest


def pair_kernel(mine_ref, got_ref, *outs):
    k = lax.axis_index("k")
    for d in range(4):
        outs[d][k] = mine_ref[d]
        outs[d][1 - k] = got_ref[d]


def finish_kernel(genes_ref, p0, p2, p1, p3, weights_ref, tiles_ref, rho_ref, trace_ref, parts_ref):
    x, k, g, c = (lax.axis_index(a) for a in AXES)
    for d, ref in enumerate((p0, p1, p2, p3)):
        for core in range(2):
            parts_ref[2 * ((x - d) & 3) + core] = ref[core]
    part = 2 * x + k
    row, lane = iota((WIDTH, WIDTH), 0), iota((WIDTH, WIDTH), 1)
    whitened = jnp.concatenate([parts_ref[t, 16:32, :] for t in range(8)], 0)
    rest = jnp.concatenate([parts_ref[t, 32:48, :] for t in range(8)], 0)
    direct = ((row < 64) & ((lane >= 64) | (row <= lane))) | ((row >= 64) & (lane >= 64) & (row > lane))
    for q in range(2):
        rank = 2 * part + q
        packed = jnp.concatenate([parts_ref[t, 8 * q:8 * q + 8, :] for t in range(8)], 0)
        full = jnp.concatenate([packed, pltpu.roll(packed, 64, 1)], 0)
        gram = jnp.where(direct, full, full.T)
        w = jnp.where((lane >> 5) == 2 * (part & 1) + q, whitened, 0.0)
        projected = lax.dot_general(w, w, (((1,), (1,)), ((), ())), precision=HIGHEST,
                                    preferred_element_type=F32)
        weight_col = jnp.sum(jnp.where(lane == 32 + rank, rest, 0.0), axis=1, keepdims=True)
        diag_col = jnp.sum(jnp.where(lane == 16 + rank, rest, 0.0), axis=1, keepdims=True)
        weight_row = weights_ref[pl.ds(rank, 1), :]
        tile = weight_col * weight_row * (gram - projected) * (1.0 / SAMPLES)
        tiles_ref[q] = jnp.where(row == lane, diag_col, tile)

    row8 = iota((8, WIDTH), 0)
    member = jnp.where(genes_ref[...] == iota((16, WIDTH), 1), 1.0, 0.0)
    none = jnp.zeros((16, WIDTH), F32)
    rest_of = jnp.zeros((WIDTH - 32, WIDTH), F32)
    squares = jnp.sum(rest * rest, axis=0, keepdims=True)
    sums = jnp.sum(rest, axis=0, keepdims=True)
    table = jnp.where(row8 == 0, squares, sums)
    by_gene = jnp.dot(table, jnp.concatenate([member, none, rest_of], 0), precision=HIGHEST,
                      preferred_element_type=F32)[:, :8]
    traces = jnp.dot(table, jnp.concatenate([none, member, rest_of], 0), precision=HIGHEST,
                     preferred_element_type=F32)[:, :8]
    level = iota((8, 8), 0)
    rho = jnp.zeros((8, 8), F32)
    for i, value in enumerate(RHO_GRID):
        rho = jnp.where(level == i, value, rho)
    burden = by_gene[1:2, :]
    rho_ref[...] = ((1.0 - rho) * by_gene[0:1, :] + rho * (burden * burden)) * (1.0 / WIDTH)
    trace_ref[...] = traces[1:2, :] * (1.0 / WIDTH)


def turns(d, first):
    pairs = []
    for x in range(4):
        for k in range(2):
            for g in range(4):
                for c in range(4):
                    along_x = (k == 0) == first
                    xd, cd = ((x + d) % 4, c) if along_x else (x, (c + d) % 4)
                    pairs.append((((x * 2 + k) * 4 + g) * 4 + c, ((xd * 2 + k) * 4 + g) * 4 + cd))
    return pairs


def shards(dosage, covariates, phenotype, sample_mask, variant_weight, bucket_owner, variant_gene):
    samples = dosage.shape[0]
    keep, send, *raw = products(bucket_owner, dosage, covariates.T, phenotype.reshape(-1, WIDTH),
                                sample_mask.reshape(1, samples))
    other = [(0, 1), (1, 0)]
    recv = lax.ppermute(send, "k", other)
    keep_cross, send_cross = vmem_call(
        cross_kernel, [jax.ShapeDtypeStruct((4, 4, CROSS, WIDTH), F32)] * 2, "cross", 3,
        scratch=[pltpu.VMEM((20, WIDTH, WIDTH), F32)])(*raw)
    recv_cross = lax.ppermute(send_cross, "k", other)
    first = [jax.ShapeDtypeStruct((4, GRAM, WIDTH), F32)] * 4
    a = vmem_call(first_sum_kernel, first, "first_sum", 2)(keep, recv)
    r = {d: lax.ppermute(a[d], AXES, turns(d, True)) for d in (2, 1, 3)}
    first = [jax.ShapeDtypeStruct((4, CROSS, WIDTH), F32)] * 4
    ac = vmem_call(first_sum_kernel, first, "cross_sum", 2)(keep_cross, recv_cross)
    rc = {d: lax.ppermute(ac[d], AXES, turns(d, True)) for d in (2, 1, 3)}
    list16 = jax.ShapeDtypeStruct((16,), jnp.int32)
    square = jax.ShapeDtypeStruct((WIDTH, WIDTH), F32)
    tile16 = jax.ShapeDtypeStruct((16, WIDTH), F32)
    turn, slot_at, source, rank, genes, scale, weights = vmem_call(
        layout_kernel, [list16] * 4 + [jax.ShapeDtypeStruct((16, WIDTH), jnp.int32)] + [tile16] * 2,
        "layout", 4, smem_in=1, smem_out=(0, 1, 2, 3), any_in=1,
        scratch=[pltpu.VMEM((WIDTH, WIDTH), F32), pltpu.VMEM((16, WIDTH), jnp.int32),
                 pltpu.SMEM((17,), jnp.int32), pltpu.SMEM((4,), jnp.int32)],
    )(bucket_owner, variant_weight.reshape(-1, WIDTH), variant_gene.reshape(-1, WIDTH), ac[0])
    part = jax.ShapeDtypeStruct((CHUNK, WIDTH), F32)
    b = vmem_call(second_sum_kernel, [part] * 4, "second_sum", 9, any_in=1)(
        a[0], r[2], r[1], r[3], ac[0], rc[2], rc[1], rc[3], weights)
    q = {d: lax.ppermute(b[d], AXES, turns(d, False)) for d in (2, 1, 3)}
    routed = jax.ShapeDtypeStruct((ROUTED, WIDTH), F32)
    *e, moment = vmem_call(
        route_kernel, [routed] * 4 + [tile16], "route", 6, smem_in=2,
        scratch=[pltpu.VMEM((CHUNK, WIDTH), F32), pltpu.VMEM((4, ROUTED, WIDTH), F32)],
    )(turn, slot_at, b[0], q[2], q[1], q[3])
    w = {d: lax.ppermute(e[d], "g", [(i, (i + d) % 4) for i in range(4)]) for d in (2, 1, 3)}
    whiten, half = vmem_call(solve_kernel, [square] * 2, "solve", 1)(moment)
    mine, theirs = vmem_call(
        scores_kernel, [jax.ShapeDtypeStruct((4, FINAL, WIDTH), F32)] * 2, "scores", 9, smem_in=2,
        scratch=[pltpu.VMEM((4, ROUTED, WIDTH), F32), pltpu.VMEM((64, WIDTH), F32)],
    )(source, rank, e[0], w[2], w[1], w[3], whiten, half, scale)
    got = lax.ppermute(theirs, "k", other)
    p = vmem_call(pair_kernel, [jax.ShapeDtypeStruct((2, FINAL, WIDTH), F32)] * 4, "pair", 2)(
        mine, got)
    p = [p[0]] + [lax.ppermute(p[d], "x", [(i, (i + d) % 4) for i in range(4)]) for d in (2, 1, 3)]
    tiles, rho, trace = vmem_call(
        finish_kernel,
        [jax.ShapeDtypeStruct((2, WIDTH, WIDTH), F32), jax.ShapeDtypeStruct((8, 8), F32),
         jax.ShapeDtypeStruct((1, 8), F32)], "finish", 6,
        scratch=[pltpu.VMEM((8, FINAL, WIDTH), F32)],
    )(genes, *p, weights)
    return tiles[None], rho, trace.reshape(8)


def solution(mesh):
    grid = Mesh(mesh.devices.reshape(4, 2, 4, 4), AXES)
    rows = ("x", "k", "c")
    owners = ("g", "c")
    return jax.shard_map(
        shards,
        mesh=grid,
        in_specs=(P(rows, "g"), P(rows, None), P(rows), P(rows), P(), P(), P()),
        out_specs=(P(owners, ("x", "k"), None, None), P(None, owners), P(owners)),
        check_vma=False,
    )
```

```python
import jax
import jax.numpy as jnp
from jax import lax
from jax.experimental import pallas as pl
from jax.experimental.pallas import tpu as pltpu
from jax.sharding import Mesh, PartitionSpec as P

AXES = ("x", "k", "g", "c")
RHO_GRID = (0.0, 0.01, 0.04, 0.09, 0.16, 0.25, 0.5, 1.0)
SAMPLES = 16384
WIDTH = 128
COVS = 32
LOCAL = 64
STEP = 16
LOAD = 16
AHEAD = 2
GRAM = 128
CROSS = 80
CHUNK = GRAM + CROSS
ROUTED = 112
FINAL = 48
F32 = jnp.float32
HIGHEST = lax.Precision.HIGHEST


def params(**kwargs):
    return pltpu.CompilerParams(vmem_limit_bytes=48 * 1024 * 1024, **kwargs)


def iota(shape, dim):
    return lax.broadcasted_iota(jnp.int32, shape, dim)


def placed(core, xd, cd):
    x, k, g, c = (lax.axis_index(a) for a in AXES)
    first = core == 0
    return jnp.where(first, (xd - x) & 3, (cd - c) & 3), jnp.where(first, cd, xd)


def products_kernel(owner_hbm, dosage_ref, cov_hbm, pheno_hbm, mask_hbm, keep_ref, send_ref,
                    cross_ref, rest_ref, moment_ref, owner_ref, cov_ref, pheno_ref, mask_ref,
                    panel_ref, left_ref, packed_ref, count_ref, sems, small_sems):
    x, k, g, c = (lax.axis_index(a) for a in AXES)
    samples = dosage_ref.shape[0]

    def fetch(i):
        at = pl.ds(pl.multiple_of(i * LOAD * WIDTH, WIDTH), LOAD * WIDTH)
        return pltpu.make_async_copy(dosage_ref.at[:, at], panel_ref.at[i], sems.at[i])

    small = [
        pltpu.make_async_copy(src, dst, small_sems.at[i])
        for i, (src, dst) in enumerate([(cov_hbm, cov_ref), (pheno_hbm, pheno_ref),
                                        (mask_hbm, mask_ref), (owner_hbm, owner_ref)])]
    for copy in small:
        copy.start()
    for i in range(AHEAD):
        fetch(i).start()

    rest_ref[...] = jnp.zeros_like(rest_ref)
    for i in range(4):
        count_ref[i] = 0
    for copy in small:
        copy.wait()
    cov_rows = cov_ref[...]
    pheno = jnp.concatenate([pheno_ref[i:i + 1, :] for i in range(samples // WIDTH)], 1)
    right = jnp.concatenate(
        [cov_rows, pheno, jnp.zeros((WIDTH - COVS - 1, cov_rows.shape[1]), jnp.bfloat16)], 0)
    keep = mask_ref[...].astype(F32).astype(jnp.bfloat16)
    masked = right[:48] * keep
    left_ref[...] = masked
    m = lax.dot_general(masked[:COVS], right, (((1,), (1,)), ((), ())),
                        preferred_element_type=F32)
    moment_ref[...] = pltpu.roll(m[:16], 32, 1) + pltpu.roll(m[16:32], 65, 1)

    keep_row = mask_ref[...].astype(F32).astype(jnp.bfloat16)
    row, lane = iota((64, WIDTH), 0), iota((64, WIDTH), 1)
    take_low = (lane < 64) & (row > lane)
    eye = iota((WIDTH, WIDTH), 0) == iota((WIDTH, WIDTH), 1)
    def run(step, _):
        for pair in range(STEP // 2):
            load = step * (STEP // LOAD) + pair * 2 // LOAD
            if pair * 2 % LOAD == 0:
                fetch(load).wait()

                @pl.when(load + AHEAD < LOCAL // LOAD)
                def _():
                    fetch(load + AHEAD).start()

            lo = pair * 256 % (LOAD * WIDTH)
            panel = panel_ref[load, :, lo:lo + 256]
            left = jnp.concatenate([panel.T * keep_row, left_ref[...]], 0)
            out = jnp.dot(left, panel, preferred_element_type=F32)
            for half in range(2):
                lo = half * WIDTH
                block = out[lo:lo + WIDTH, lo:lo + WIDTH]
                bucket = step * STEP + pair * 2 + half
                cd = owner_ref[g * LOCAL + bucket] & 3
                pos = count_ref[cd]
                count_ref[cd] = pos + 1
                slot = pair * 2 + half
                packed_ref[slot] = jnp.where(take_low, pltpu.roll(block[64:], 64, 1), block[:64])
                rows = pl.ds(pl.multiple_of(pos * 8, 8), 8)
                for xd in range(4):
                    d, j = placed(k, xd, cd)
                    keep_ref[d, j, rows, :] = packed_ref[
                        slot, pl.ds(pl.multiple_of((2 * xd + k) * 8, 8), 8), :]
                    d, j = placed(1 - k, xd, cd)
                    send_ref[d, j, rows, :] = packed_ref[
                        slot, pl.ds(pl.multiple_of((2 * xd + 1 - k) * 8, 8), 8), :]
                cross_ref[cd, pl.ds(pl.multiple_of(pos * COVS, 8), COVS), :] = out[
                    256:256 + COVS, lo:lo + WIDTH]
                rest_ref[cd, pl.ds(pos, 1), :] = out[256 + COVS:257 + COVS, lo:lo + WIDTH]
                rest_ref[cd, pl.ds(pos + 16, 1), :] = jnp.sum(
                    jnp.where(eye, block, 0.0), axis=0, keepdims=True)
        return 0

    lax.fori_loop(0, LOCAL // STEP, run, 0)


def cross_kernel(cross_ref, rest_ref, moment_ref, keep_ref, send_ref, turned_ref):
    k = lax.axis_index("k")
    for cd in range(4):
        for q in range(5):
            slot = cd * 5 + q
            if q < 4:
                turned_ref[slot] = cross_ref[cd, q * WIDTH:(q + 1) * WIDTH, :].T
            else:
                moment = moment_ref[...]
                turned_ref[slot] = rest_ref[cd].T + jnp.concatenate([moment] * 8, 0)
            for xd in range(4):
                for core, ref in ((k, keep_ref), (1 - k, send_ref)):
                    d, j = placed(core, xd, cd)
                    at = pl.ds(pl.multiple_of((2 * xd + core) * 16, 16), 16)
                    ref[d, j, 16 * q:16 * q + 16, :] = turned_ref[slot, at, :]


def products(owner, dosage, cov, pheno, mask):
    samples = dosage.shape[0]
    vmem = pl.BlockSpec(memory_space=pltpu.VMEM)
    shapes = [(4, 4, GRAM, WIDTH)] * 2 + [(4, 16 * COVS, WIDTH), (4, WIDTH, WIDTH), (16, WIDTH)]
    return pl.pallas_call(
        products_kernel,
        out_shape=tuple(jax.ShapeDtypeStruct(shape, F32) for shape in shapes),
        in_specs=[pl.BlockSpec(memory_space=pltpu.HBM)] * 5,
        out_specs=(vmem,) * 5,
        scratch_shapes=[
            pltpu.SMEM(owner.shape, jnp.int32),
            pltpu.VMEM(cov.shape, jnp.bfloat16),
            pltpu.VMEM(pheno.shape, jnp.bfloat16),
            pltpu.VMEM(mask.shape, jnp.int32),
            pltpu.VMEM((LOCAL // LOAD, samples, LOAD * WIDTH), jnp.bfloat16),
            pltpu.VMEM((48, samples), jnp.bfloat16),
            pltpu.VMEM((STEP, 64, WIDTH), F32),
            pltpu.SMEM((4,), jnp.int32),
            pltpu.SemaphoreType.DMA((LOCAL // LOAD,)),
            pltpu.SemaphoreType.DMA((4,)),
        ],
        compiler_params=params(),
        name="products",
    )(*[pltpu.with_memory_space_constraint(a, pltpu.HBM)
        for a in (owner, dosage, cov, pheno, mask)])


def far_sum_kernel(keep_ref, recv_ref, out):
    out[...] = keep_ref[2] + recv_ref[2]


def near_sum_kernel(keep_ref, recv_ref, keep_cross_ref, recv_cross_ref, _, a0, a1, a3, c2):
    for d, out in ((0, a0), (1, a1), (3, a3)):
        out[:, :GRAM, :] = keep_ref[d] + recv_ref[d]
        out[:, GRAM:, :] = keep_cross_ref[d] + recv_cross_ref[d]
    c2[...] = keep_cross_ref[2] + recv_cross_ref[2]


def second_sum_kernel(a0, a2, c2, a1, a3, _, *outs):
    x, k, g, c = (lax.axis_index(a) for a in AXES)
    base = jnp.where(k == 0, c, x)
    for d in range(4):
        j = (base + d) & 3
        outs[d][:GRAM] = (a0[j, :GRAM] + a1[j, :GRAM]) + (a2[j] + a3[j, :GRAM])
        outs[d][GRAM:] = (a0[j, GRAM:] + a1[j, GRAM:]) + (c2[j] + a3[j, GRAM:])


def vmem_call(kernel, shapes, name, n_in, scratch=(), smem_in=0, smem_out=(), any_in=0):
    specs = [pl.BlockSpec(memory_space=pltpu.SMEM)] * smem_in + [
        pl.BlockSpec(memory_space=pltpu.VMEM)] * (n_in - smem_in - any_in) + [
        pl.BlockSpec(memory_space=pl.ANY)] * any_in
    return pl.pallas_call(
        kernel,
        out_shape=tuple(shapes),
        in_specs=specs,
        out_specs=tuple(
            pl.BlockSpec(memory_space=pltpu.SMEM if i in smem_out else pltpu.VMEM)
            for i in range(len(shapes))),
        scratch_shapes=scratch,
        compiler_params=params(),
        name=name,
    )


def route_kernel(turn_ref, slot_at_ref, b0, q2, q1, q3, e0, e1, e2, e3, moment_ref, total_ref,
                 slot_ref):
    total_ref[...] = (b0[...] + q1[...]) + (q2[...] + q3[...])
    rest = total_ref[192:208, :]
    moment_ref[...] = rest
    slot_ref[...] = jnp.zeros_like(slot_ref)
    lane = iota((16, WIDTH), 1)
    for pos in range(16):
        d, pr = turn_ref[pos], slot_at_ref[pos]
        slot_ref[d, pl.ds(pl.multiple_of(pr * 8, 8), 8), :] = total_ref[8 * pos:8 * pos + 8, :]
        tile = total_ref[128 + 16 * (pos >> 2):144 + 16 * (pos >> 2), :]
        tile = pltpu.roll(tile, (32 * (pr - pos)) & 127, 1)
        at = pl.ds(pl.multiple_of(64 + 16 * (pr >> 2), 16), 16)
        slot_ref[d, at, :] = jnp.where((lane >> 5) == (pr & 3), tile, slot_ref[d, at, :])
        slot_ref[d, 96:112, :] = jnp.where(
            (lane == pr) | (lane == pr + 16), pltpu.roll(rest, (pr - pos) & 127, 1),
            slot_ref[d, 96:112, :])
    for d, out in enumerate((e0, e1, e2, e3)):
        out[...] = slot_ref[d]


def layout_kernel(owner_ref, weight_ref, gene_ref, _, turn_ref, slot_at_ref, source_ref, rank_ref,
                  genes_ref, scale_ref, weights_ref, pad_ref, label_ref, list_ref, count_ref):
    x, k, g, c = (lax.axis_index(a) for a in AXES)
    me = g * 4 + c
    for i in range(4):
        count_ref[i] = 0
    pad_ref[...] = jnp.zeros_like(pad_ref)

    def scan(start, count, wanted, list_ref, value):
        def body(i, end):
            for u in range(8):
                bucket = start + i * 8 + u
                owner = owner_ref[bucket]
                list_ref[end] = value(bucket, owner)
                end = end + wanted(owner).astype(jnp.int32)
            return end

        lax.fori_loop(0, count // 8, body, 0)

    scan(g * LOCAL, LOCAL, lambda owner: (owner & 3) == c, list_ref, lambda b, owner: owner >> 2)
    for pos in range(16):
        gd = list_ref[pos]
        pr = count_ref[gd]
        count_ref[gd] = pr + 1
        turn_ref[pos] = (gd - g) & 3
        slot_at_ref[pos] = pr
    scan(0, 4 * LOCAL, lambda owner: owner == me, list_ref, lambda b, owner: b)
    last, pr = -1, 0
    for r in range(16):
        bucket = list_ref[r]
        source = bucket >> 6
        pr = jnp.where(source == last, pr + 1, 0)
        last = source
        source_ref[r] = (g - source) & 3
        rank_ref[r] = pr
        genes = gene_ref[pl.ds(bucket, 1), :]
        pad_ref[r:r + 1, :] = jnp.where(genes >= 0, weight_ref[pl.ds(bucket, 1), :], 0.0)
        label_ref[r:r + 1, :] = genes
    labels = jnp.max(label_ref[...], axis=1, keepdims=True)
    genes_ref[...] = jnp.broadcast_to(labels - me * 8, genes_ref.shape)

    weights_ref[...] = pad_ref[:16, :]
    pad_ref[...] = pad_ref[...].T
    mine = pad_ref[pl.ds(pl.multiple_of((2 * x + k) * 16, 16), 16), :]
    by16 = pltpu.roll(mine, 16, 1)
    scale_ref[...] = (mine * (1.0 / 128.0) + by16 * by16 * (1.0 / SAMPLES)
                      + pltpu.roll(mine, 32, 1))


def solve_kernel(moment_ref, whiten_ref, half_ref):
    m = moment_ref[...]
    m = jnp.concatenate([pltpu.roll(m, WIDTH - 32, 1), pltpu.roll(m, WIDTH - 65, 1)], 0)
    row, lane = iota((COVS, WIDTH), 0), iota((COVS, WIDTH), 1)
    m = jnp.where(lane <= COVS, m, jnp.where(lane == row + 64, 1.0, 0.0))
    first = jnp.zeros((COVS, WIDTH), F32)
    mixed = jnp.zeros((COVS, WIDTH), F32)
    second = jnp.ones((COVS, WIDTH), F32)
    for i in range(0, COVS, 2):
        col0 = jnp.broadcast_to(m[:, i:i + 1], m.shape)
        col1 = jnp.broadcast_to(m[:, i + 1:i + 2], m.shape)
        a, b, d = col0[i:i + 1, :], col0[i + 1:i + 2, :], col1[i + 1:i + 2, :]
        inv = 1.0 / (a * d - b * b)
        below = row > i + 1
        first = jnp.where(row >= i, a, first)
        mixed = jnp.where(row == i + 1, b, mixed)
        second = jnp.where(row == i, a, jnp.where(row == i + 1, d, second))
        m = (m - jnp.where(below, (col0 * d - col1 * b) * inv, 0.0) * m[i:i + 1, :]
             - jnp.where(below, (col1 * a - col0 * b) * inv, 0.0) * m[i + 1:i + 2, :])
    ratio = mixed / first
    m = (m - ratio * pltpu.roll(m, 1, 0)) * lax.rsqrt(second - mixed * ratio)
    inverse = jnp.where(lane < COVS, pltpu.roll(m, 64, 1), 0.0)
    whiten_ref[...] = jnp.concatenate(
        [inverse] + [pltpu.roll(inverse, 32 * q, 1) for q in range(1, 4)], 0)
    half = jnp.concatenate([jnp.broadcast_to(m[:, COVS:COVS + 1], m.shape)] * 4, 0)
    row, lane = iota((WIDTH, WIDTH), 0), iota((WIDTH, WIDTH), 1)
    half_ref[...] = jnp.where(lane == (row >> 5), half, 0.0)


def scores_kernel(source_ref, rank_ref, w0, w3, w2, w1, whiten_ref, half_ref, scale_ref,
                  mine_ref, other_ref, slot_ref, cross_ref):
    x, k = lax.axis_index("x"), lax.axis_index("k")
    for d, ref in enumerate((w0, w1, w2, w3)):
        slot_ref[d] = ref[...]
    lane = iota((16, WIDTH), 1)
    rest = jnp.zeros((16, WIDTH), F32)
    for group in range(4):
        tile = jnp.zeros((16, WIDTH), F32)
        for q in range(4):
            r = group * 4 + q
            d, pr = source_ref[r], rank_ref[r]
            part = slot_ref[d, pl.ds(pl.multiple_of(64 + 16 * (pr >> 2), 16), 16), :]
            part = pltpu.roll(part, (32 * (q - pr)) & 127, 1)
            tile = jnp.where((lane >> 5) == q, part, tile)
            more = pltpu.roll(slot_ref[d, 96:112, :], (r - pr) & 127, 1)
            rest = jnp.where((lane == r) | (lane == r + 16), more, rest)
        cross_ref[group * 16:group * 16 + 16, :] = tile
    whitened = lax.dot_general(cross_ref[...], whiten_ref[...], (((1,), (1,)), ((), ())),
                               precision=HIGHEST, preferred_element_type=F32)
    row, col = iota((WIDTH, WIDTH), 0), iota((WIDTH, WIDTH), 1)
    ones = jnp.where(col == (row >> 5) + 16, 1.0, 0.0)
    taken = (jnp.dot(whitened, half_ref[...], precision=HIGHEST, preferred_element_type=F32)
             + jnp.dot(whitened * whitened, ones, precision=HIGHEST, preferred_element_type=F32))
    for group in range(4):
        rest = rest - pltpu.roll(taken[group * 16:group * 16 + 16], 4 * group, 1)
    scale = scale_ref[...]
    rest = jnp.where(lane < 32, rest * scale, jnp.where(lane < 48, scale, 0.0))
    cross_ref[...] = whitened
    for d in range(4):
        xd = (x + d) & 3
        for core, ref in ((k, mine_ref), (1 - k, other_ref)):
            for q in range(2):
                r = 4 * xd + 2 * core + q
                ref[d, 8 * q:8 * q + 8, :] = slot_ref[
                    source_ref[r], pl.ds(pl.multiple_of(rank_ref[r] * 8, 8), 8), :]
            ref[d, 16:32, :] = cross_ref[pl.ds(pl.multiple_of(16 * xd, 16), 16), :]
            ref[d, 32:48, :] = rest


def pair_kernel(mine_ref, got_ref, *outs):
    k = lax.axis_index("k")
    for d in range(4):
        outs[d][k] = mine_ref[d]
        outs[d][1 - k] = got_ref[d]


def finish_kernel(genes_ref, p0, p2, p1, p3, weights_ref, tiles_ref, rho_ref, trace_ref, parts_ref):
    x, k, g, c = (lax.axis_index(a) for a in AXES)
    for d, ref in enumerate((p0, p1, p2, p3)):
        for core in range(2):
            parts_ref[2 * ((x - d) & 3) + core] = ref[core]
    part = 2 * x + k
    row, lane = iota((WIDTH, WIDTH), 0), iota((WIDTH, WIDTH), 1)
    whitened = jnp.concatenate([parts_ref[t, 16:32, :] for t in range(8)], 0)
    rest = jnp.concatenate([parts_ref[t, 32:48, :] for t in range(8)], 0)
    direct = ((row < 64) & ((lane >= 64) | (row <= lane))) | ((row >= 64) & (lane >= 64) & (row > lane))
    for q in range(2):
        rank = 2 * part + q
        packed = jnp.concatenate([parts_ref[t, 8 * q:8 * q + 8, :] for t in range(8)], 0)
        full = jnp.concatenate([packed, pltpu.roll(packed, 64, 1)], 0)
        gram = jnp.where(direct, full, full.T)
        w = jnp.where((lane >> 5) == 2 * (part & 1) + q, whitened, 0.0)
        projected = lax.dot_general(w, w, (((1,), (1,)), ((), ())), precision=HIGHEST,
                                    preferred_element_type=F32)
        weight_col = jnp.sum(jnp.where(lane == 32 + rank, rest, 0.0), axis=1, keepdims=True)
        diag_col = jnp.sum(jnp.where(lane == 16 + rank, rest, 0.0), axis=1, keepdims=True)
        weight_row = weights_ref[pl.ds(rank, 1), :]
        tile = weight_col * weight_row * (gram - projected) * (1.0 / SAMPLES)
        tiles_ref[q] = jnp.where(row == lane, diag_col, tile)

    row8 = iota((8, WIDTH), 0)
    member = jnp.where(genes_ref[...] == iota((16, WIDTH), 1), 1.0, 0.0)
    none = jnp.zeros((16, WIDTH), F32)
    rest_of = jnp.zeros((WIDTH - 32, WIDTH), F32)
    squares = jnp.sum(rest * rest, axis=0, keepdims=True)
    sums = jnp.sum(rest, axis=0, keepdims=True)
    table = jnp.where(row8 == 0, squares, sums)
    by_gene = jnp.dot(table, jnp.concatenate([member, none, rest_of], 0), precision=HIGHEST,
                      preferred_element_type=F32)[:, :8]
    traces = jnp.dot(table, jnp.concatenate([none, member, rest_of], 0), precision=HIGHEST,
                     preferred_element_type=F32)[:, :8]
    level = iota((8, 8), 0)
    rho = jnp.zeros((8, 8), F32)
    for i, value in enumerate(RHO_GRID):
        rho = jnp.where(level == i, value, rho)
    burden = by_gene[1:2, :]
    rho_ref[...] = ((1.0 - rho) * by_gene[0:1, :] + rho * (burden * burden)) * (1.0 / WIDTH)
    trace_ref[...] = traces[1:2, :] * (1.0 / WIDTH)


def turns(d, first):
    pairs = []
    for x in range(4):
        for k in range(2):
            for g in range(4):
                for c in range(4):
                    along_x = (k == 0) == first
                    xd, cd = ((x + d) % 4, c) if along_x else (x, (c + d) % 4)
                    pairs.append((((x * 2 + k) * 4 + g) * 4 + c, ((xd * 2 + k) * 4 + g) * 4 + cd))
    return pairs


def shards(dosage, covariates, phenotype, sample_mask, variant_weight, bucket_owner, variant_gene):
    samples = dosage.shape[0]
    keep, send, *raw = products(bucket_owner, dosage, covariates.T, phenotype.reshape(-1, WIDTH),
                                sample_mask.reshape(1, samples))
    other = [(0, 1), (1, 0)]
    recv = lax.ppermute(send, "k", other)
    keep_cross, send_cross = vmem_call(
        cross_kernel, [jax.ShapeDtypeStruct((4, 4, CROSS, WIDTH), F32)] * 2, "cross", 3,
        scratch=[pltpu.VMEM((20, WIDTH, WIDTH), F32)])(*raw)
    recv_cross = lax.ppermute(send_cross, "k", other)
    gram = jax.ShapeDtypeStruct((4, GRAM, WIDTH), F32)
    (far,) = vmem_call(far_sum_kernel, [gram], "far_sum", 2)(keep, recv)
    a2 = lax.ppermute(far, AXES, turns(2, True))
    chunk = jax.ShapeDtypeStruct((4, CHUNK, WIDTH), F32)
    rest = jax.ShapeDtypeStruct((4, CROSS, WIDTH), F32)
    a0, a1, a3, far_cross = vmem_call(near_sum_kernel, [chunk] * 3 + [rest], "near_sum", 5, any_in=1)(
        keep, recv, keep_cross, recv_cross, far)
    a1 = lax.ppermute(a1, AXES, turns(1, True))
    a3 = lax.ppermute(a3, AXES, turns(3, True))
    c2 = lax.ppermute(far_cross, AXES, turns(2, True))
    list16 = jax.ShapeDtypeStruct((16,), jnp.int32)
    square = jax.ShapeDtypeStruct((WIDTH, WIDTH), F32)
    tile16 = jax.ShapeDtypeStruct((16, WIDTH), F32)
    turn, slot_at, source, rank, genes, scale, weights = vmem_call(
        layout_kernel, [list16] * 4 + [jax.ShapeDtypeStruct((16, WIDTH), jnp.int32)] + [tile16] * 2,
        "layout", 4, smem_in=1, smem_out=(0, 1, 2, 3), any_in=1,
        scratch=[pltpu.VMEM((WIDTH, WIDTH), F32), pltpu.VMEM((16, WIDTH), jnp.int32),
                 pltpu.SMEM((17,), jnp.int32), pltpu.SMEM((4,), jnp.int32)],
    )(bucket_owner, variant_weight.reshape(-1, WIDTH), variant_gene.reshape(-1, WIDTH), a0)
    part = jax.ShapeDtypeStruct((CHUNK, WIDTH), F32)
    b = vmem_call(second_sum_kernel, [part] * 4, "second_sum", 6, any_in=1)(
        a0, a2, c2, a1, a3, weights)
    q = {d: lax.ppermute(b[d], AXES, turns(d, False)) for d in (2, 1, 3)}
    routed = jax.ShapeDtypeStruct((ROUTED, WIDTH), F32)
    *e, moment = vmem_call(
        route_kernel, [routed] * 4 + [tile16], "route", 6, smem_in=2,
        scratch=[pltpu.VMEM((CHUNK, WIDTH), F32), pltpu.VMEM((4, ROUTED, WIDTH), F32)],
    )(turn, slot_at, b[0], q[2], q[1], q[3])
    w = {d: lax.ppermute(e[d], "g", [(i, (i + d) % 4) for i in range(4)]) for d in (2, 1, 3)}
    whiten, half = vmem_call(solve_kernel, [square] * 2, "solve", 1)(moment)
    mine, theirs = vmem_call(
        scores_kernel, [jax.ShapeDtypeStruct((4, FINAL, WIDTH), F32)] * 2, "scores", 9, smem_in=2,
        scratch=[pltpu.VMEM((4, ROUTED, WIDTH), F32), pltpu.VMEM((64, WIDTH), F32)],
    )(source, rank, e[0], w[3], w[2], w[1], whiten, half, scale)
    got = lax.ppermute(theirs, "k", other)
    p = vmem_call(pair_kernel, [jax.ShapeDtypeStruct((2, FINAL, WIDTH), F32)] * 4, "pair", 2)(
        mine, got)
    p = [p[0]] + [lax.ppermute(p[d], "x", [(i, (i + d) % 4) for i in range(4)]) for d in (2, 1, 3)]
    tiles, rho, trace = vmem_call(
        finish_kernel,
        [jax.ShapeDtypeStruct((2, WIDTH, WIDTH), F32), jax.ShapeDtypeStruct((8, 8), F32),
         jax.ShapeDtypeStruct((1, 8), F32)], "finish", 6,
        scratch=[pltpu.VMEM((8, FINAL, WIDTH), F32)],
    )(genes, *p, weights)
    return tiles[None], rho, trace.reshape(8)


def solution(mesh):
    grid = Mesh(mesh.devices.reshape(4, 2, 4, 4), AXES)
    rows = ("x", "k", "c")
    owners = ("g", "c")
    return jax.shard_map(
        shards,
        mesh=grid,
        in_specs=(P(rows, "g"), P(rows, None), P(rows), P(rows), P(), P(), P()),
        out_specs=(P(owners, ("x", "k"), None, None), P(None, owners), P(owners)),
        check_vma=False,
    )
```

```python
import jax
import jax.numpy as jnp
from jax import lax
from jax.experimental import pallas as pl
from jax.experimental.pallas import tpu as pltpu
from jax.sharding import Mesh, PartitionSpec as P

AXES = ("x", "k", "g", "c")
RHO_GRID = (0.0, 0.01, 0.04, 0.09, 0.16, 0.25, 0.5, 1.0)
SAMPLES = 16384
WIDTH = 128
COVS = 32
LOCAL = 64
STEP = 16
LOAD = 16
AHEAD = 2
GRAM = 128
CROSS = 80
CHUNK = GRAM + CROSS
ROUTED = 112
FINAL = 48
F32 = jnp.float32
HIGHEST = lax.Precision.HIGHEST


def params(**kwargs):
    return pltpu.CompilerParams(vmem_limit_bytes=48 * 1024 * 1024, **kwargs)


def iota(shape, dim):
    return lax.broadcasted_iota(jnp.int32, shape, dim)


def placed(core, xd, cd):
    x, k, g, c = (lax.axis_index(a) for a in AXES)
    first = core == 0
    return jnp.where(first, (xd - x) & 3, (cd - c) & 3), jnp.where(first, cd, xd)


def products_kernel(owner_hbm, dosage_ref, cov_hbm, pheno_hbm, mask_hbm, keep_ref, send_ref,
                    cross_ref, rest_ref, moment_ref, owner_ref, cov_ref, pheno_ref, mask_ref,
                    panel_ref, left_ref, packed_ref, count_ref, sems, small_sems):
    x, k, g, c = (lax.axis_index(a) for a in AXES)
    samples = dosage_ref.shape[0]

    def fetch(i):
        at = pl.ds(pl.multiple_of(i * LOAD * WIDTH, WIDTH), LOAD * WIDTH)
        return pltpu.make_async_copy(dosage_ref.at[:, at], panel_ref.at[i], sems.at[i])

    small = [
        pltpu.make_async_copy(src, dst, small_sems.at[i])
        for i, (src, dst) in enumerate([(cov_hbm, cov_ref), (pheno_hbm, pheno_ref),
                                        (mask_hbm, mask_ref), (owner_hbm, owner_ref)])]
    for copy in small:
        copy.start()
    for i in range(AHEAD):
        fetch(i).start()

    rest_ref[...] = jnp.zeros_like(rest_ref)
    for i in range(4):
        count_ref[i] = 0
    for copy in small:
        copy.wait()
    cov_rows = cov_ref[...]
    pheno = jnp.concatenate([pheno_ref[i:i + 1, :] for i in range(samples // WIDTH)], 1)
    right = jnp.concatenate(
        [cov_rows, pheno, jnp.zeros((WIDTH - COVS - 1, cov_rows.shape[1]), jnp.bfloat16)], 0)
    keep = mask_ref[...].astype(F32).astype(jnp.bfloat16)
    masked = right[:48] * keep
    left_ref[...] = masked
    m = lax.dot_general(masked[:COVS], right, (((1,), (1,)), ((), ())),
                        preferred_element_type=F32)
    moment_ref[...] = pltpu.roll(m[:16], 32, 1) + pltpu.roll(m[16:32], 65, 1)

    keep_row = mask_ref[...].astype(F32).astype(jnp.bfloat16)
    row, lane = iota((64, WIDTH), 0), iota((64, WIDTH), 1)
    take_low = (lane < 64) & (row > lane)
    eye = iota((WIDTH, WIDTH), 0) == iota((WIDTH, WIDTH), 1)
    def run(step, _):
        for pair in range(STEP // 2):
            load = step * (STEP // LOAD) + pair * 2 // LOAD
            if pair * 2 % LOAD == 0:
                fetch(load).wait()

                @pl.when(load + AHEAD < LOCAL // LOAD)
                def _():
                    fetch(load + AHEAD).start()

            lo = pair * 256 % (LOAD * WIDTH)
            panel = panel_ref[load, :, lo:lo + 256]
            left = jnp.concatenate([panel.T * keep_row, left_ref[...]], 0)
            out = jnp.dot(left, panel, preferred_element_type=F32)
            for half in range(2):
                lo = half * WIDTH
                block = out[lo:lo + WIDTH, lo:lo + WIDTH]
                bucket = step * STEP + pair * 2 + half
                cd = owner_ref[g * LOCAL + bucket] & 3
                pos = count_ref[cd]
                count_ref[cd] = pos + 1
                slot = pair * 2 + half
                packed_ref[slot] = jnp.where(take_low, pltpu.roll(block[64:], 64, 1), block[:64])
                rows = pl.ds(pl.multiple_of(pos * 8, 8), 8)
                for xd in range(4):
                    d, j = placed(k, xd, cd)
                    keep_ref[d, j, rows, :] = packed_ref[
                        slot, pl.ds(pl.multiple_of((2 * xd + k) * 8, 8), 8), :]
                    d, j = placed(1 - k, xd, cd)
                    send_ref[d, j, rows, :] = packed_ref[
                        slot, pl.ds(pl.multiple_of((2 * xd + 1 - k) * 8, 8), 8), :]
                cross_ref[cd, pl.ds(pl.multiple_of(pos * COVS, 8), COVS), :] = out[
                    256:256 + COVS, lo:lo + WIDTH]
                rest_ref[cd, pl.ds(pos, 1), :] = out[256 + COVS:257 + COVS, lo:lo + WIDTH]
                rest_ref[cd, pl.ds(pos + 16, 1), :] = jnp.sum(
                    jnp.where(eye, block, 0.0), axis=0, keepdims=True)
        return 0

    lax.fori_loop(0, LOCAL // STEP, run, 0)


def cross_kernel(cross_ref, rest_ref, moment_ref, keep_ref, send_ref, turned_ref):
    k = lax.axis_index("k")
    for cd in range(4):
        for q in range(5):
            slot = cd * 5 + q
            if q < 4:
                turned_ref[slot] = cross_ref[cd, q * WIDTH:(q + 1) * WIDTH, :].T
            else:
                moment = moment_ref[...]
                turned_ref[slot] = rest_ref[cd].T + jnp.concatenate([moment] * 8, 0)
            for xd in range(4):
                for core, ref in ((k, keep_ref), (1 - k, send_ref)):
                    d, j = placed(core, xd, cd)
                    at = pl.ds(pl.multiple_of((2 * xd + core) * 16, 16), 16)
                    ref[d, j, 16 * q:16 * q + 16, :] = turned_ref[slot, at, :]


def products(owner, dosage, cov, pheno, mask):
    samples = dosage.shape[0]
    vmem = pl.BlockSpec(memory_space=pltpu.VMEM)
    shapes = [(4, 4, GRAM, WIDTH)] * 2 + [(4, 16 * COVS, WIDTH), (4, WIDTH, WIDTH), (16, WIDTH)]
    return pl.pallas_call(
        products_kernel,
        out_shape=tuple(jax.ShapeDtypeStruct(shape, F32) for shape in shapes),
        in_specs=[pl.BlockSpec(memory_space=pltpu.HBM)] * 5,
        out_specs=(vmem,) * 5,
        scratch_shapes=[
            pltpu.SMEM(owner.shape, jnp.int32),
            pltpu.VMEM(cov.shape, jnp.bfloat16),
            pltpu.VMEM(pheno.shape, jnp.bfloat16),
            pltpu.VMEM(mask.shape, jnp.int32),
            pltpu.VMEM((LOCAL // LOAD, samples, LOAD * WIDTH), jnp.bfloat16),
            pltpu.VMEM((48, samples), jnp.bfloat16),
            pltpu.VMEM((STEP, 64, WIDTH), F32),
            pltpu.SMEM((4,), jnp.int32),
            pltpu.SemaphoreType.DMA((LOCAL // LOAD,)),
            pltpu.SemaphoreType.DMA((4,)),
        ],
        compiler_params=params(),
        name="products",
    )(*[pltpu.with_memory_space_constraint(a, pltpu.HBM)
        for a in (owner, dosage, cov, pheno, mask)])


def far_sum_kernel(keep_ref, recv_ref, out):
    out[...] = keep_ref[2] + recv_ref[2]


def near_sum_kernel(keep_ref, recv_ref, keep_cross_ref, recv_cross_ref, _, a0, a1, a3, c2):
    for d, out in ((0, a0), (1, a1), (3, a3)):
        out[:, :GRAM, :] = keep_ref[d] + recv_ref[d]
        out[:, GRAM:, :] = keep_cross_ref[d] + recv_cross_ref[d]
    c2[...] = keep_cross_ref[2] + recv_cross_ref[2]


def second_sum_kernel(a0, a2, c2, a1, a3, _, *outs):
    x, k, g, c = (lax.axis_index(a) for a in AXES)
    base = jnp.where(k == 0, c, x)
    for d in range(4):
        j = (base + d) & 3
        outs[d][:GRAM] = (a0[j, :GRAM] + a1[j, :GRAM]) + (a2[j] + a3[j, :GRAM])
        outs[d][GRAM:] = (a0[j, GRAM:] + a1[j, GRAM:]) + (c2[j] + a3[j, GRAM:])


def vmem_call(kernel, shapes, name, n_in, scratch=(), smem_in=0, smem_out=(), any_in=0):
    specs = [pl.BlockSpec(memory_space=pltpu.SMEM)] * smem_in + [
        pl.BlockSpec(memory_space=pltpu.VMEM)] * (n_in - smem_in - any_in) + [
        pl.BlockSpec(memory_space=pl.ANY)] * any_in
    return pl.pallas_call(
        kernel,
        out_shape=tuple(shapes),
        in_specs=specs,
        out_specs=tuple(
            pl.BlockSpec(memory_space=pltpu.SMEM if i in smem_out else pltpu.VMEM)
            for i in range(len(shapes))),
        scratch_shapes=scratch,
        compiler_params=params(),
        name=name,
    )


def route_kernel(turn_ref, slot_at_ref, b0, q2, q1, q3, e0, e1, e2, e3, moment_ref, total_ref,
                 slot_ref):
    total_ref[...] = (b0[...] + q1[...]) + (q2[...] + q3[...])
    rest = total_ref[192:208, :]
    moment_ref[...] = rest
    slot_ref[...] = jnp.zeros_like(slot_ref)
    lane = iota((16, WIDTH), 1)
    for pos in range(16):
        d, pr = turn_ref[pos], slot_at_ref[pos]
        slot_ref[d, pl.ds(pl.multiple_of(pr * 8, 8), 8), :] = total_ref[8 * pos:8 * pos + 8, :]
        tile = total_ref[128 + 16 * (pos >> 2):144 + 16 * (pos >> 2), :]
        tile = pltpu.roll(tile, (32 * (pr - pos)) & 127, 1)
        at = pl.ds(pl.multiple_of(64 + 16 * (pr >> 2), 16), 16)
        slot_ref[d, at, :] = jnp.where((lane >> 5) == (pr & 3), tile, slot_ref[d, at, :])
        slot_ref[d, 96:112, :] = jnp.where(
            (lane == pr) | (lane == pr + 16), pltpu.roll(rest, (pr - pos) & 127, 1),
            slot_ref[d, 96:112, :])
    for d, out in enumerate((e0, e1, e2, e3)):
        out[...] = slot_ref[d]


def layout_kernel(owner_ref, weight_ref, gene_ref, _, turn_ref, slot_at_ref, source_ref, rank_ref,
                  genes_ref, scale_ref, weights_ref, pad_ref, label_ref, list_ref, count_ref):
    x, k, g, c = (lax.axis_index(a) for a in AXES)
    me = g * 4 + c
    for i in range(4):
        count_ref[i] = 0
    pad_ref[...] = jnp.zeros_like(pad_ref)

    def scan(start, count, wanted, list_ref, value):
        def body(i, end):
            for u in range(8):
                bucket = start + i * 8 + u
                owner = owner_ref[bucket]
                list_ref[end] = value(bucket, owner)
                end = end + wanted(owner).astype(jnp.int32)
            return end

        lax.fori_loop(0, count // 8, body, 0)

    scan(g * LOCAL, LOCAL, lambda owner: (owner & 3) == c, list_ref, lambda b, owner: owner >> 2)
    for pos in range(16):
        gd = list_ref[pos]
        pr = count_ref[gd]
        count_ref[gd] = pr + 1
        turn_ref[pos] = (gd - g) & 3
        slot_at_ref[pos] = pr
    scan(0, 4 * LOCAL, lambda owner: owner == me, list_ref, lambda b, owner: b)
    last, pr = -1, 0
    for r in range(16):
        bucket = list_ref[r]
        source = bucket >> 6
        pr = jnp.where(source == last, pr + 1, 0)
        last = source
        source_ref[r] = (g - source) & 3
        rank_ref[r] = pr
        genes = gene_ref[pl.ds(bucket, 1), :]
        pad_ref[r:r + 1, :] = jnp.where(genes >= 0, weight_ref[pl.ds(bucket, 1), :], 0.0)
        label_ref[r:r + 1, :] = genes
    labels = jnp.max(label_ref[...], axis=1, keepdims=True)
    genes_ref[...] = jnp.broadcast_to(labels - me * 8, genes_ref.shape)

    weights_ref[...] = pad_ref[:16, :]
    pad_ref[...] = pad_ref[...].T
    mine = pad_ref[pl.ds(pl.multiple_of((2 * x + k) * 16, 16), 16), :]
    by16 = pltpu.roll(mine, 16, 1)
    scale_ref[...] = (mine * (1.0 / 128.0) + by16 * by16 * (1.0 / SAMPLES)
                      + pltpu.roll(mine, 32, 1))


def solve_kernel(moment_ref, whiten_ref, half_ref):
    m = moment_ref[...]
    m = jnp.concatenate([pltpu.roll(m, WIDTH - 32, 1), pltpu.roll(m, WIDTH - 65, 1)], 0)
    row, lane = iota((COVS, WIDTH), 0), iota((COVS, WIDTH), 1)
    m = jnp.where(lane <= COVS, m, jnp.where(lane == row + 64, 1.0, 0.0))
    first = jnp.zeros((COVS, WIDTH), F32)
    mixed = jnp.zeros((COVS, WIDTH), F32)
    second = jnp.ones((COVS, WIDTH), F32)
    for i in range(0, COVS, 2):
        col0 = jnp.broadcast_to(m[:, i:i + 1], m.shape)
        col1 = jnp.broadcast_to(m[:, i + 1:i + 2], m.shape)
        a, b, d = col0[i:i + 1, :], col0[i + 1:i + 2, :], col1[i + 1:i + 2, :]
        inv = 1.0 / (a * d - b * b)
        below = row > i + 1
        first = jnp.where(row >= i, a, first)
        mixed = jnp.where(row == i + 1, b, mixed)
        second = jnp.where(row == i, a, jnp.where(row == i + 1, d, second))
        m = (m - jnp.where(below, (col0 * d - col1 * b) * inv, 0.0) * m[i:i + 1, :]
             - jnp.where(below, (col1 * a - col0 * b) * inv, 0.0) * m[i + 1:i + 2, :])
    ratio = mixed / first
    m = (m - ratio * pltpu.roll(m, 1, 0)) * lax.rsqrt(second - mixed * ratio)
    inverse = jnp.where(lane < COVS, pltpu.roll(m, 64, 1), 0.0)
    whiten_ref[...] = jnp.concatenate(
        [inverse] + [pltpu.roll(inverse, 32 * q, 1) for q in range(1, 4)], 0)
    half = jnp.concatenate([jnp.broadcast_to(m[:, COVS:COVS + 1], m.shape)] * 4, 0)
    row, lane = iota((WIDTH, WIDTH), 0), iota((WIDTH, WIDTH), 1)
    half_ref[...] = jnp.where(lane == (row >> 5), half, 0.0)


def scores_kernel(source_ref, rank_ref, w0, w3, w2, w1, whiten_ref, half_ref, scale_ref,
                  mine_ref, other_ref, slot_ref, cross_ref):
    x, k = lax.axis_index("x"), lax.axis_index("k")
    for d, ref in enumerate((w0, w1, w2, w3)):
        slot_ref[d] = ref[...]
    lane = iota((16, WIDTH), 1)
    rest = jnp.zeros((16, WIDTH), F32)
    for group in range(4):
        tile = jnp.zeros((16, WIDTH), F32)
        for q in range(4):
            r = group * 4 + q
            d, pr = source_ref[r], rank_ref[r]
            part = slot_ref[d, pl.ds(pl.multiple_of(64 + 16 * (pr >> 2), 16), 16), :]
            part = pltpu.roll(part, (32 * (q - pr)) & 127, 1)
            tile = jnp.where((lane >> 5) == q, part, tile)
            more = pltpu.roll(slot_ref[d, 96:112, :], (r - pr) & 127, 1)
            rest = jnp.where((lane == r) | (lane == r + 16), more, rest)
        cross_ref[group * 16:group * 16 + 16, :] = tile
    whitened = lax.dot_general(cross_ref[...], whiten_ref[...], (((1,), (1,)), ((), ())),
                               precision=HIGHEST, preferred_element_type=F32)
    row, col = iota((WIDTH, WIDTH), 0), iota((WIDTH, WIDTH), 1)
    ones = jnp.where(col == (row >> 5) + 16, 1.0, 0.0)
    taken = jnp.dot(jnp.concatenate([whitened, whitened * whitened], 1),
                    jnp.concatenate([half_ref[...], ones], 0), precision=HIGHEST,
                    preferred_element_type=F32)
    for group in range(4):
        rest = rest - pltpu.roll(taken[group * 16:group * 16 + 16], 4 * group, 1)
    scale = scale_ref[...]
    rest = jnp.where(lane < 32, rest * scale, jnp.where(lane < 48, scale, 0.0))
    cross_ref[...] = whitened
    for d in range(4):
        xd = (x + d) & 3
        for core, ref in ((k, mine_ref), (1 - k, other_ref)):
            for q in range(2):
                r = 4 * xd + 2 * core + q
                ref[d, 8 * q:8 * q + 8, :] = slot_ref[
                    source_ref[r], pl.ds(pl.multiple_of(rank_ref[r] * 8, 8), 8), :]
            ref[d, 16:32, :] = cross_ref[pl.ds(pl.multiple_of(16 * xd, 16), 16), :]
            ref[d, 32:48, :] = rest


def pair_kernel(mine_ref, got_ref, *outs):
    k = lax.axis_index("k")
    for d in range(4):
        outs[d][k] = mine_ref[d]
        outs[d][1 - k] = got_ref[d]


def finish_kernel(genes_ref, p0, p2, p1, p3, weights_ref, tiles_ref, rho_ref, trace_ref, parts_ref):
    x, k, g, c = (lax.axis_index(a) for a in AXES)
    for d, ref in enumerate((p0, p1, p2, p3)):
        for core in range(2):
            parts_ref[2 * ((x - d) & 3) + core] = ref[core]
    part = 2 * x + k
    row, lane = iota((WIDTH, WIDTH), 0), iota((WIDTH, WIDTH), 1)
    whitened = jnp.concatenate([parts_ref[t, 16:32, :] for t in range(8)], 0)
    rest = jnp.concatenate([parts_ref[t, 32:48, :] for t in range(8)], 0)
    direct = ((row < 64) & ((lane >= 64) | (row <= lane))) | ((row >= 64) & (lane >= 64) & (row > lane))
    for q in range(2):
        rank = 2 * part + q
        packed = jnp.concatenate([parts_ref[t, 8 * q:8 * q + 8, :] for t in range(8)], 0)
        full = jnp.concatenate([packed, pltpu.roll(packed, 64, 1)], 0)
        gram = jnp.where(direct, full, full.T)
        w = jnp.where((lane >> 5) == 2 * (part & 1) + q, whitened, 0.0)
        projected = lax.dot_general(w, w, (((1,), (1,)), ((), ())), precision=HIGHEST,
                                    preferred_element_type=F32)
        weight_col = jnp.sum(jnp.where(lane == 32 + rank, rest, 0.0), axis=1, keepdims=True)
        diag_col = jnp.sum(jnp.where(lane == 16 + rank, rest, 0.0), axis=1, keepdims=True)
        weight_row = weights_ref[pl.ds(rank, 1), :]
        tile = weight_col * weight_row * (gram - projected) * (1.0 / SAMPLES)
        tiles_ref[q] = jnp.where(row == lane, diag_col, tile)

    row8 = iota((8, WIDTH), 0)
    member = jnp.where(genes_ref[...] == iota((16, WIDTH), 1), 1.0, 0.0)
    member = jnp.concatenate(
        [member, pltpu.roll(member, 8, 1), jnp.zeros((WIDTH - 32, WIDTH), F32)], 0)
    squares = jnp.sum(rest * rest, axis=0, keepdims=True)
    sums = jnp.sum(rest, axis=0, keepdims=True)
    table = jnp.where(row8 == 0, squares, sums)
    totals = jnp.dot(table, member, precision=HIGHEST, preferred_element_type=F32)
    by_gene, traces = totals[:, :8], totals[:, 8:16]
    level = iota((8, 8), 0)
    rho = jnp.zeros((8, 8), F32)
    for i, value in enumerate(RHO_GRID):
        rho = jnp.where(level == i, value, rho)
    burden = by_gene[1:2, :]
    rho_ref[...] = ((1.0 - rho) * by_gene[0:1, :] + rho * (burden * burden)) * (1.0 / WIDTH)
    trace_ref[...] = traces[1:2, :] * (1.0 / WIDTH)


def turns(d, first):
    pairs = []
    for x in range(4):
        for k in range(2):
            for g in range(4):
                for c in range(4):
                    along_x = (k == 0) == first
                    xd, cd = ((x + d) % 4, c) if along_x else (x, (c + d) % 4)
                    pairs.append((((x * 2 + k) * 4 + g) * 4 + c, ((xd * 2 + k) * 4 + g) * 4 + cd))
    return pairs


def shards(dosage, covariates, phenotype, sample_mask, variant_weight, bucket_owner, variant_gene):
    samples = dosage.shape[0]
    keep, send, *raw = products(bucket_owner, dosage, covariates.T, phenotype.reshape(-1, WIDTH),
                                sample_mask.reshape(1, samples))
    other = [(0, 1), (1, 0)]
    recv = lax.ppermute(send, "k", other)
    keep_cross, send_cross = vmem_call(
        cross_kernel, [jax.ShapeDtypeStruct((4, 4, CROSS, WIDTH), F32)] * 2, "cross", 3,
        scratch=[pltpu.VMEM((20, WIDTH, WIDTH), F32)])(*raw)
    recv_cross = lax.ppermute(send_cross, "k", other)
    gram = jax.ShapeDtypeStruct((4, GRAM, WIDTH), F32)
    (far,) = vmem_call(far_sum_kernel, [gram], "far_sum", 2)(keep, recv)
    a2 = lax.ppermute(far, AXES, turns(2, True))
    chunk = jax.ShapeDtypeStruct((4, CHUNK, WIDTH), F32)
    rest = jax.ShapeDtypeStruct((4, CROSS, WIDTH), F32)
    a0, a1, a3, far_cross = vmem_call(near_sum_kernel, [chunk] * 3 + [rest], "near_sum", 5, any_in=1)(
        keep, recv, keep_cross, recv_cross, far)
    a1 = lax.ppermute(a1, AXES, turns(1, True))
    a3 = lax.ppermute(a3, AXES, turns(3, True))
    c2 = lax.ppermute(far_cross, AXES, turns(2, True))
    list16 = jax.ShapeDtypeStruct((16,), jnp.int32)
    square = jax.ShapeDtypeStruct((WIDTH, WIDTH), F32)
    tile16 = jax.ShapeDtypeStruct((16, WIDTH), F32)
    turn, slot_at, source, rank, genes, scale, weights = vmem_call(
        layout_kernel, [list16] * 4 + [jax.ShapeDtypeStruct((16, WIDTH), jnp.int32)] + [tile16] * 2,
        "layout", 4, smem_in=1, smem_out=(0, 1, 2, 3), any_in=1,
        scratch=[pltpu.VMEM((WIDTH, WIDTH), F32), pltpu.VMEM((16, WIDTH), jnp.int32),
                 pltpu.SMEM((17,), jnp.int32), pltpu.SMEM((4,), jnp.int32)],
    )(bucket_owner, variant_weight.reshape(-1, WIDTH), variant_gene.reshape(-1, WIDTH), a0)
    part = jax.ShapeDtypeStruct((CHUNK, WIDTH), F32)
    b = vmem_call(second_sum_kernel, [part] * 4, "second_sum", 6, any_in=1)(
        a0, a2, c2, a1, a3, weights)
    q = {d: lax.ppermute(b[d], AXES, turns(d, False)) for d in (2, 1, 3)}
    routed = jax.ShapeDtypeStruct((ROUTED, WIDTH), F32)
    *e, moment = vmem_call(
        route_kernel, [routed] * 4 + [tile16], "route", 6, smem_in=2,
        scratch=[pltpu.VMEM((CHUNK, WIDTH), F32), pltpu.VMEM((4, ROUTED, WIDTH), F32)],
    )(turn, slot_at, b[0], q[2], q[1], q[3])
    w = {d: lax.ppermute(e[d], "g", [(i, (i + d) % 4) for i in range(4)]) for d in (2, 1, 3)}
    whiten, half = vmem_call(solve_kernel, [square] * 2, "solve", 1)(moment)
    mine, theirs = vmem_call(
        scores_kernel, [jax.ShapeDtypeStruct((4, FINAL, WIDTH), F32)] * 2, "scores", 9, smem_in=2,
        scratch=[pltpu.VMEM((4, ROUTED, WIDTH), F32), pltpu.VMEM((64, WIDTH), F32)],
    )(source, rank, e[0], w[3], w[2], w[1], whiten, half, scale)
    got = lax.ppermute(theirs, "k", other)
    p = vmem_call(pair_kernel, [jax.ShapeDtypeStruct((2, FINAL, WIDTH), F32)] * 4, "pair", 2)(
        mine, got)
    p = [p[0]] + [lax.ppermute(p[d], "x", [(i, (i + d) % 4) for i in range(4)]) for d in (2, 1, 3)]
    tiles, rho, trace = vmem_call(
        finish_kernel,
        [jax.ShapeDtypeStruct((2, WIDTH, WIDTH), F32), jax.ShapeDtypeStruct((8, 8), F32),
         jax.ShapeDtypeStruct((1, 8), F32)], "finish", 6,
        scratch=[pltpu.VMEM((8, FINAL, WIDTH), F32)],
    )(genes, *p, weights)
    return tiles[None], rho, trace.reshape(8)


def solution(mesh):
    grid = Mesh(mesh.devices.reshape(4, 2, 4, 4), AXES)
    rows = ("x", "k", "c")
    owners = ("g", "c")
    return jax.shard_map(
        shards,
        mesh=grid,
        in_specs=(P(rows, "g"), P(rows, None), P(rows), P(rows), P(), P(), P()),
        out_specs=(P(owners, ("x", "k"), None, None), P(None, owners), P(owners)),
        check_vma=False,
    )
```
